32 devices in a mesh: table: 16 (over z, y, core), dp: 2 (over x).
Axes of the slice: x: 2, y: 2, z: 4, core: 2. Of those that a mesh axis runs over, the one named last changes fastest.
Arguments:
- owners: int32 [16384, 8], P(('table', 'dp')), may hold values from 0 to 15, all different within a row; in each aligned block of 512 rows (0 to 511, 512 to 1023, ...) at most 512 rows name the same one
- local_rows: int32 [16384, 8], P(('table', 'dp')), may hold values from 0 to 4095
- grad_pooled: bfloat16 [16384, 128], P(('table', 'dp')), may hold values from -4 to 4
- table: float32 [65536, 128], P('table'), may hold values from -6 to 6
- accum: float32 [65536], P('table'), may hold values from 0.1 to 4
- parity: float32 [8192, 128], P('table'), may hold values from -6 to 6
- parity_slot: int32 [65536], P('table'), may hold values from 0 to 8191, as said below
Outputs:
- pooled: bfloat16 [16384, 128], P(('table', 'dp'))
- new_table: float32 [65536, 128], P('table')
- new_accum: float32 [65536], P('table')
- new_parity: float32 [8192, 128], P('table')
The draws below stay inside these ranges and needn't reach their ends.
Inputs may be any that keep to these rules, and one draw needn't show every extreme that they name: `owners`: each bag names 8 different table devices. Among the 512 bags of one device (aligned blocks of rows), no table device is named by more than 512 bags, and in some blocks one is named by exactly 512. `parity_slot`: within the 4096 rows of one table device the values are distinct, and each device's rows include the value 8192 - 1. Parity row v is held by the table device v // 512.
All inputs are finite; a program needn't handle non-finite values.
Results may differ from the reference program's by a relative error of at most 0.0085.
Values may be sent and summed in bfloat16 or wider, within the bound.
No kernel may reach another device: no remote copies, remote signals or barrier semaphores. Data moves between devices by JAX's collectives and lax.ppermute only.
A program may use at most 64 MiB of HBM per device.

```python
import math
import jax
import jax.numpy as jnp
import numpy as np
from jax import lax

E = 128
HOT = 8
B_DEV = 512
R_DEV = 4096
CAP = 512
PSLOTS = 8192
ROWS = 65536
BAGS = 16384
N_TABLE = 16


def draw_parity_slot(key, part):
    device_keys = jax.random.split(key, ROWS // R_DEV)

    def one_device(device_key):
        chosen = jax.random.permutation(device_key, PSLOTS)[:R_DEV]
        present = jnp.any(chosen == PSLOTS - 1)
        return chosen.at[0].set(jnp.where(present, chosen[0], PSLOTS - 1))
    return jax.vmap(one_device)(device_keys).reshape(ROWS).astype(jnp.int32)


def touch_ends(result, key, smallest, high):
    longest = result.shape.index(max(result.shape))
    spots = []
    for shift in (0, 1):
        where = [jax.random.randint(jax.random.fold_in(key, axis), (), 0, length) for axis, length in enumerate(result.shape)]
        where[longest] = (where[longest] + shift) % result.shape[longest]
        spots.append(tuple(where))
    return result.at[spots[0]].set(smallest).at[spots[1]].set(high)


def steps_of(key, extent, shards, least, top_value):
    def one(dim, shards_of):
        draws = jax.random.uniform(jax.random.fold_in(jax.random.fold_in(key, 6), dim), (shards_of,), jnp.float32, least / len(shards), top_value / len(shards))
        return jnp.repeat(jnp.exp(draws), extent[dim] // shards_of).reshape((-1,) + (1,) * (len(extent) - dim - 1))

    level = one(*shards[0])
    for cut in shards[1:]:
        level = level * one(*cut)
    return level


def assign_block(rng, own, number, rows, count, top, bound, slope):
    ranking = jax.random.permutation(rng, count)
    heavy_load, ordinary = shares(count, rows * top, bound, slope, True), shares(count, rows * top, bound, slope, False)
    places = jnp.arange(count)

    def named(tallies, offset_by):
        used = int((tallies > 0).sum())
        fixed = max(1, used // 4)
        shifted = fixed + (places - fixed + offset_by * (used - fixed)) % max(1, count - fixed)
        return jnp.zeros((count,), jnp.int32).at[ranking[jnp.where(places < fixed, places, shifted)]].set(jnp.asarray(tallies, jnp.int32))

    tallies = jnp.where(number % 4 == 0, named(heavy_load, number // 4), named(ordinary, number - number // 4 - 1))
    mixed = jax.random.permutation(jax.random.fold_in(own, 3), count)
    giver, receiver = mixed[0:count // 2 * 2:2], mixed[1:count // 2 * 2:2]
    margin = jnp.minimum(tallies[giver] - 1, bound - tallies[receiver]) // 2
    margin = jnp.where((giver == ranking[0]) | (receiver == ranking[0]) | (tallies[receiver] == 0), 0, jnp.maximum(margin, 0))
    shifted = jax.random.randint(jax.random.fold_in(own, 4), (count // 2,), 0, 1 << 20) % (margin + 1)
    tallies = tallies.at[giver].add(-shifted).at[receiver].add(shifted)
    labels = jnp.searchsorted(jnp.cumsum(tallies), jnp.arange(rows * top), side="right").astype(jnp.int32)
    listing = labels.reshape(top, rows).T
    listing = listing[jax.random.permutation(jax.random.fold_in(own, 1), rows)]
    offset_by = jax.random.randint(jax.random.fold_in(own, 2), (rows, 1), 0, top)
    return jnp.take_along_axis(listing, (jnp.arange(top)[None, :] + offset_by) % top, axis=1)


def shares(amount, total, most, lean, full):
    weights = [(1 << 20) // math.isqrt(grade ** lean) + 1 for grade in range(1, amount + 1)]
    largest = most if full else min(most, max(-(-total // amount), total * weights[0] // sum(weights)))
    least = 1 if total - largest >= amount - 1 else 0
    given, surplus = [largest] + [least] * (amount - 1), total - largest - least * (amount - 1)
    while surplus > 0:
        free = [i for i in range(1, amount) if given[i] < largest] or [i for i in range(1, amount) if given[i] < most]
        pool, left = sum([weights[i] for i in free]), surplus
        for i in free:
            extra = min(most - given[i], max(1, left * weights[i] // pool), surplus)
            given[i] = given[i] + extra
            surplus = surplus - extra
    return np.array(given)


def noise(key, shape, scale, most, cuts=(), dtype=jnp.bfloat16):
    factor_of = steps_of(key, shape, cuts, -0.22, 0.18) if cuts else 1.0
    result = jax.random.normal(key, shape, jnp.float32) * scale * factor_of
    return jnp.minimum(jnp.maximum(result, -most), most).astype(dtype)


def setup_inputs(seed: int = 0) -> dict:
    key_list = jax.random.split(jax.random.key(seed), 8)
    owners_keys = jax.random.split(jax.random.fold_in(key_list[0], 1), BAGS // B_DEV)
    owners_turns = jax.random.permutation(jax.random.fold_in(key_list[0], 3), BAGS // B_DEV)
    owners = jax.vmap(lambda own, number: assign_block(jax.random.fold_in(key_list[0], 2), own, number, B_DEV, N_TABLE, HOT, CAP, 1))(owners_keys, owners_turns).reshape((BAGS, HOT))
    local_rows = touch_ends(jax.random.randint(key_list[1], (BAGS, HOT), 0, R_DEV), jax.random.fold_in(key_list[1], 1), 0, R_DEV - 1).astype(jnp.int32)
    grad_pooled = noise(key_list[2], (BAGS, E), 0.5, 4.0, ((0, 32),))
    table = noise(key_list[3], (ROWS, E), 1.0, 6.0, ((0, 16),), jnp.float32)
    accum = jnp.clip(jnp.exp(math.log(4.0) - 3.6888794 * jax.random.uniform(key_list[4], (ROWS,), jnp.float32) ** steps_of(key_list[4], (ROWS,), ((0, 16),), -0.2, 0.2)), 0.1, 4.0)
    parity = noise(key_list[5], (PSLOTS, E), 1.0, 6.0, ((0, 16),), jnp.float32)
    parity_slot = draw_parity_slot(jax.random.fold_in(key_list[7], 71), 0)
    return {"owners": owners, "local_rows": local_rows, "grad_pooled": grad_pooled, "table": table, "accum": accum, "parity": parity, "parity_slot": parity_slot}


LEARN = 0.5
EPSILON = 1e-06

def reference(owners, local_rows, grad_pooled, table, accum, parity, parity_slot):
    row_index = (owners * R_DEV + local_rows).astype(jnp.int32)
    table_half = table.astype(jnp.bfloat16)
    pooled = jnp.zeros((BAGS, E), jnp.float32)
    row_grads = jnp.zeros((ROWS, E), jnp.float32)
    bag_grads = grad_pooled.astype(jnp.float32)
    for lookup in range(HOT):
        pooled = pooled + table_half[row_index[:, lookup]].astype(jnp.float32)
        row_grads = row_grads.at[row_index[:, lookup]].add(bag_grads)
    new_accum = accum + lax.optimization_barrier(jnp.mean(row_grads * row_grads, axis=1))
    new_table = table - LEARN * row_grads / jnp.sqrt(new_accum + EPSILON)[:, None]
    row_delta = new_table - table
    new_parity = parity + jax.ops.segment_sum(row_delta, parity_slot, num_segments=PSLOTS)
    return (pooled.astype(jnp.bfloat16), new_table, new_accum, new_parity)
```

```python
import functools
import jax
import jax.numpy as jnp
from jax import lax
from jax.experimental import pallas as pl
from jax.experimental.pallas import tpu as pltpu
from jax.sharding import PartitionSpec as P

LEARN = 0.5
EPSILON = 1e-06
SPLIT = 4


def column_of(row, lanes):
    return jnp.broadcast_to(row, (lanes, row.shape[1])).T


def split_index(index, low_count):
    bits = low_count.bit_length() - 1
    return lax.shift_right_arithmetic(index, bits), lax.bitwise_and(index, low_count - 1)


def tile_of(count, most):
    tile = most
    while count % tile:
        tile //= 2
    return tile


def segment_kernel(index_ref, rows_ref, out_ref, total_ref, *, low_count):
    step = pl.program_id(0)
    index = index_ref[0]
    width = rows_ref.shape[1]
    block, low = split_index(index, low_count)
    low = jnp.where(index < 0, -1, low)
    hits = (
        (lax.broadcasted_iota(jnp.int32, (low_count, index.shape[1]), 0) == low)
        .astype(jnp.float32)
        .astype(jnp.bfloat16)
    )
    block_column = column_of(block, width)
    rows = rows_ref[...].astype(jnp.float32)
    spread = jnp.concatenate(
        [jnp.where(block_column == i, rows, 0.0).astype(jnp.bfloat16) for i in range(SPLIT)], axis=1
    )
    part = jnp.dot(hits, spread, preferred_element_type=jnp.float32)

    @pl.when(step == 0)
    def _():
        total_ref[...] = part

    @pl.when(step > 0)
    def _():
        total_ref[...] += part

    @pl.when(step == pl.num_programs(0) - 1)
    def _():
        for i in range(SPLIT):
            out_ref[i] = total_ref[:, i * width : (i + 1) * width].astype(out_ref.dtype)


def segment_sums(index, rows, segment_count):
    count, width = rows.shape
    tile = tile_of(count, 2048)
    low_count = segment_count // SPLIT
    out = pl.pallas_call(
        functools.partial(segment_kernel, low_count=low_count),
        grid=(count // tile,),
        in_specs=[
            pl.BlockSpec((1, 1, tile), lambda k: (k, 0, 0)),
            pl.BlockSpec((tile, width), lambda k: (k, 0)),
        ],
        out_specs=pl.BlockSpec((SPLIT, low_count, width), lambda k: (0, 0, 0)),
        out_shape=jax.ShapeDtypeStruct((SPLIT, low_count, width), jnp.bfloat16),
        scratch_shapes=[pltpu.VMEM((low_count, SPLIT * width), jnp.float32)],
    )(index.reshape(count // tile, 1, tile), rows)
    return out.reshape(segment_count, width)


def gather_kernel(own_index_ref, peer_index_ref, own_ref, peer_ref, out_ref, held_ref, *, low_count):
    width = out_ref.shape[1]

    @pl.when(pl.program_id(0) == 0)
    def _():
        for i in range(SPLIT):
            held_ref[0, :, i * width : (i + 1) * width] = own_ref[i]
            held_ref[1, :, i * width : (i + 1) * width] = peer_ref[i]

    total = jnp.zeros(out_ref.shape, jnp.float32)
    lane = lax.broadcasted_iota(jnp.int32, out_ref.shape, 1)
    for side, index_ref in enumerate((own_index_ref, peer_index_ref)):
        block, low = split_index(column_of(index_ref[0], width), low_count)
        hits = jnp.concatenate(
            [
                (lane == low - first).astype(jnp.float32).astype(jnp.bfloat16)
                for first in range(0, low_count, width)
            ],
            axis=1,
        )
        found = jnp.dot(hits, held_ref[side], preferred_element_type=jnp.float32)
        for i in range(SPLIT):
            total += jnp.where(block == i, found[:, i * width : (i + 1) * width], 0.0)
    out_ref[...] = total.astype(out_ref.dtype)


def gather_pair_sums(own_index, peer_index, own_rows, peer_rows):
    count = own_index.size
    row_count, width = own_rows.shape
    tile = tile_of(count, 1024)
    low_count = row_count // SPLIT
    index_spec = pl.BlockSpec((1, 1, tile), lambda k: (k, 0, 0))
    rows_spec = pl.BlockSpec((SPLIT, low_count, width), lambda k: (0, 0, 0))
    return pl.pallas_call(
        functools.partial(gather_kernel, low_count=low_count),
        grid=(count // tile,),
        in_specs=[index_spec, index_spec, rows_spec, rows_spec],
        out_specs=pl.BlockSpec((tile, width), lambda k: (k, 0)),
        out_shape=jax.ShapeDtypeStruct((count, width), jnp.bfloat16),
        scratch_shapes=[pltpu.VMEM((2, low_count, SPLIT * width), jnp.bfloat16)],
    )(
        own_index.reshape(count // tile, 1, tile),
        peer_index.reshape(count // tile, 1, tile),
        own_rows.reshape(SPLIT, low_count, width),
        peer_rows.reshape(SPLIT, low_count, width),
    )


def on_device(owners, local_rows, grad_pooled, table, accum, parity, parity_slot):
    table_count = lax.axis_size("table")
    dp_count = lax.axis_size("dp")
    chip_count = table_count // 2
    bag_count = owners.shape[0]
    row_count, row_width = table.shape
    parity_count = parity.shape[0]
    core = lax.axis_index("table") % 2
    dp_index = lax.axis_index("dp")
    pairs = [(i, i ^ 1) for i in range(table_count)]
    same_core = [list(range(c, table_count, 2)) for c in range(2)]

    def swap_cores(values):
        return lax.ppermute(values, "table", pairs)

    def exchange(values):
        return lax.all_to_all(
            values, "table", split_axis=0, concat_axis=0, axis_index_groups=same_core, tiled=True
        )

    sent_grads = jnp.broadcast_to(grad_pooled[None], (chip_count, bag_count, row_width))
    own_grads = exchange(sent_grads)
    devices = jnp.arange(table_count, dtype=jnp.int32)[:, None, None]
    named = owners.T[None] == devices.reshape(table_count, 1, 1)
    requests = jnp.max(jnp.where(named, local_rows.T[None], -1), axis=1)
    asked = exchange(requests.reshape(chip_count, 2, bag_count))
    asked_own = jnp.where(core == 0, asked[:, 0], asked[:, 1])
    asked_other = jnp.where(core == 0, asked[:, 1], asked[:, 0])
    asked_by_peer = swap_cores(asked_other)
    table_half = table.astype(jnp.bfloat16)
    peer_half = swap_cores(table_half)
    peer_slot = swap_cores(parity_slot)

    fetched = gather_pair_sums(asked_own, asked_other, table_half, peer_half)

    peer_grads = swap_cores(own_grads)
    all_grads = jnp.concatenate([own_grads, peer_grads], axis=0).reshape(-1, row_width)
    all_asked = jnp.concatenate([asked_own, asked_by_peer], axis=0).reshape(-1)
    total = segment_sums(all_asked, all_grads, row_count)
    distance = 1
    while distance < dp_count:
        step_pairs = [(i, i ^ distance) for i in range(dp_count)]
        total = total.astype(jnp.bfloat16)
        total = total.astype(jnp.float32) + lax.ppermute(total, "dp", step_pairs).astype(jnp.float32)
        distance *= 2
    row_grads = total.astype(jnp.float32)

    returned = exchange(fetched.reshape(chip_count, bag_count, row_width))
    pooled = jnp.sum(returned.astype(jnp.float32), axis=0).astype(jnp.bfloat16)

    new_accum = accum + jnp.mean(row_grads * row_grads, axis=1)
    new_table = table - LEARN * row_grads / jnp.sqrt(new_accum + EPSILON)[:, None]
    row_delta = (new_table - table).astype(jnp.bfloat16)

    part_count = parity_count // dp_count
    slots = jnp.concatenate([parity_slot, peer_slot])
    holder, offset = slots // parity_count, slots % parity_count
    mine = (holder % 2 == core) & (offset // part_count == dp_index)
    target = jnp.where(mine, holder // 2 * part_count + offset % part_count, -1)
    deltas = jnp.concatenate([row_delta, swap_cores(row_delta)], axis=0)
    changes = segment_sums(target, deltas, chip_count * part_count)
    arrived = exchange(changes.reshape(chip_count, part_count, row_width))
    part = jnp.sum(arrived.astype(jnp.float32), axis=0).astype(jnp.bfloat16)
    if dp_count == 2:
        other = lax.ppermute(part, "dp", [(0, 1), (1, 0)])
        parts = jnp.where(dp_index == 0, jnp.stack([part, other]), jnp.stack([other, part]))
    else:
        parts = lax.all_gather(part, "dp", axis=0)
    new_parity = parity + parts.reshape(parity_count, row_width).astype(jnp.float32)
    return (pooled, new_table, new_accum, new_parity)


def solution(mesh):
    in_specs = (
        P(("table", "dp"), None),
        P(("table", "dp"), None),
        P(("table", "dp"), None),
        P("table", None),
        P("table"),
        P("table", None),
        P("table"),
    )
    out_specs = (P(("table", "dp"), None), P("table", None), P("table"), P("table", None))
    return jax.shard_map(
        on_device, mesh=mesh, in_specs=in_specs, out_specs=out_specs, check_vma=False
    )
```

```python
import functools
import jax
import jax.numpy as jnp
from jax import lax
from jax.experimental import pallas as pl
from jax.experimental.pallas import tpu as pltpu
from jax.sharding import PartitionSpec as P

LEARN = 0.5
EPSILON = 1e-06
SPLIT = 4
PARTS = 2


def column_of(row, lanes):
    return jnp.broadcast_to(row, (lanes, row.shape[1])).T


def split_index(index, low_count):
    bits = low_count.bit_length() - 1
    return lax.shift_right_arithmetic(index, bits), lax.bitwise_and(index, low_count - 1)


def tile_of(count, most):
    tile = most
    while count % tile:
        tile //= 2
    return tile


def lane_row(ref, first, count):
    return jnp.concatenate([ref[pl.ds(first + i, 1), :] for i in range(count)], axis=1)


def segment_kernel(*refs, low_count, index_rows, base, sides, start_given):
    index_refs, refs = refs[:sides], refs[sides:]
    row_refs, refs = refs[:sides], refs[sides:]
    out_ref, total_ref = refs[-2:]
    step = pl.program_id(0)
    width = row_refs[0].shape[1]
    index = jnp.concatenate(
        [lane_row(ref, step * index_rows, index_rows) for ref in index_refs], axis=1
    )
    block, low = split_index(index - base, low_count)
    low = jnp.where((block < 0) | (block >= SPLIT), -1, low)
    hits = (
        (lax.broadcasted_iota(jnp.int32, (low_count, index.shape[1]), 0) == low)
        .astype(jnp.float32)
        .astype(jnp.bfloat16)
    )
    block_column = column_of(block, width)
    rows = jnp.concatenate([ref[...] for ref in row_refs], axis=0).astype(jnp.float32)
    spread = jnp.concatenate(
        [jnp.where(block_column == i, rows, 0.0).astype(jnp.bfloat16) for i in range(SPLIT)], axis=1
    )
    part = jnp.dot(hits, spread, preferred_element_type=jnp.float32)

    @pl.when(step == 0)
    def _():
        if start_given:
            for i in range(SPLIT):
                lanes = slice(i * width, (i + 1) * width)
                total_ref[:, lanes] = part[:, lanes] + refs[0][i]
        else:
            total_ref[...] = part

    @pl.when(step > 0)
    def _():
        total_ref[...] += part

    @pl.when(step == pl.num_programs(0) - 1)
    def _():
        for i in range(SPLIT):
            out_ref[i] = total_ref[:, i * width : (i + 1) * width].astype(out_ref.dtype)


def segment_sums(indices, rows, base, segment_count, dtype, start=None):
    sides = len(indices)
    index_shape = indices[0].shape
    width = rows[0].shape[1]
    low_count = segment_count // SPLIT
    index_rows = tile_of(index_shape[0], max(1, 2048 // sides // index_shape[1]))
    tile = index_rows * index_shape[1]
    block = pl.BlockSpec((SPLIT, low_count, width), lambda k: (0, 0, 0))
    given = [] if start is None else [start]
    return pl.pallas_call(
        functools.partial(
            segment_kernel,
            low_count=low_count,
            index_rows=index_rows,
            base=base,
            sides=sides,
            start_given=bool(given),
        ),
        grid=(index_shape[0] // index_rows,),
        in_specs=[pl.BlockSpec(index_shape, lambda k: (0, 0))] * sides
        + [pl.BlockSpec((tile, width), lambda k: (k, 0))] * sides
        + [block] * len(given),
        out_specs=block,
        out_shape=jax.ShapeDtypeStruct((SPLIT, low_count, width), dtype),
        scratch_shapes=[pltpu.VMEM((low_count, SPLIT * width), jnp.float32)],
    )(*indices, *rows, *given)


def gather_kernel(own_index_ref, peer_index_ref, own_ref, peer_ref, out_ref, held_ref, *, low_count, index_rows):
    width = out_ref.shape[1]
    step = pl.program_id(0)

    @pl.when(step == 0)
    def _():
        for i in range(SPLIT):
            held_ref[0, :, i * width : (i + 1) * width] = own_ref[i]
            held_ref[1, :, i * width : (i + 1) * width] = peer_ref[i]

    total = jnp.zeros(out_ref.shape, jnp.float32)
    lane = lax.broadcasted_iota(jnp.int32, out_ref.shape, 1)
    for side, index_ref in enumerate((own_index_ref, peer_index_ref)):
        index = lane_row(index_ref, step * index_rows, index_rows)
        block, low = split_index(column_of(index, width), low_count)
        hits = jnp.concatenate(
            [
                (lane == low - first).astype(jnp.float32).astype(jnp.bfloat16)
                for first in range(0, low_count, width)
            ],
            axis=1,
        )
        found = jnp.dot(hits, held_ref[side], preferred_element_type=jnp.float32)
        for i in range(SPLIT):
            total += jnp.where(block == i, found[:, i * width : (i + 1) * width], 0.0)
    out_ref[...] = total.astype(out_ref.dtype)


def gather_pair_sums(own_index, peer_index, own_rows, peer_rows):
    row_count, width = own_rows.shape
    low_count = row_count // SPLIT
    index_rows = tile_of(own_index.shape[0], max(1, 1024 // own_index.shape[1]))
    tile = index_rows * own_index.shape[1]
    index_spec = pl.BlockSpec(own_index.shape, lambda k: (0, 0))
    rows_spec = pl.BlockSpec((SPLIT, low_count, width), lambda k: (0, 0, 0))
    return pl.pallas_call(
        functools.partial(gather_kernel, low_count=low_count, index_rows=index_rows),
        grid=(own_index.shape[0] // index_rows,),
        in_specs=[index_spec, index_spec, rows_spec, rows_spec],
        out_specs=pl.BlockSpec((tile, width), lambda k: (k, 0)),
        out_shape=jax.ShapeDtypeStruct((own_index.size, width), jnp.bfloat16),
        scratch_shapes=[pltpu.VMEM((2, low_count, SPLIT * width), jnp.bfloat16)],
    )(
        own_index,
        peer_index,
        own_rows.reshape(SPLIT, low_count, width),
        peer_rows.reshape(SPLIT, low_count, width),
    )


def update_kernel(own_ref, other_ref, table_ref, accum_ref, *refs, first_line):
    new_table_ref, new_accum_ref, delta_ref = refs[-3:]
    rows, width = table_ref.shape
    lines = rows // width
    step = pl.program_id(0)
    for j in range(lines):
        at = slice(j * width, (j + 1) * width)
        grads = own_ref[at, :].astype(jnp.float32) + other_ref[at, :].astype(jnp.float32)
        old_accum = column_of(accum_ref[pl.ds(first_line + step * lines + j, 1), :], width)
        fresh_accum = old_accum + jnp.mean(grads * grads, axis=1, keepdims=True)
        old_rows = table_ref[at, :]
        fresh_rows = old_rows - LEARN * grads / jnp.sqrt(fresh_accum + EPSILON)
        new_table_ref[at, :] = fresh_rows
        delta_ref[at, :] = (fresh_rows - old_rows).astype(jnp.bfloat16)
        new_accum_ref[pl.ds(step * lines + j, 1), :] = fresh_accum.T[0:1, :]


def update(own, other, table, accum, part, unfinished):
    _, width = table.shape
    part_rows = own.shape[0]
    tile = tile_of(part_rows, 512)
    steps = part_rows // tile
    rows_spec = pl.BlockSpec((tile, width), lambda k: (k, 0))
    table_spec = pl.BlockSpec((tile, width), lambda k: (part * steps + k, 0))
    part_lines = part_rows // width
    given = [] if unfinished is None else [unfinished]
    return pl.pallas_call(
        functools.partial(update_kernel, first_line=part * part_lines),
        grid=(steps,),
        in_specs=[rows_spec, rows_spec, table_spec, pl.BlockSpec(accum.shape, lambda k: (0, 0))]
        + [pl.BlockSpec(memory_space=pl.ANY)] * len(given),
        out_specs=[table_spec, pl.BlockSpec((part_lines, width), lambda k: (0, 0)), rows_spec],
        out_shape=[
            jax.ShapeDtypeStruct(table.shape, jnp.float32),
            jax.ShapeDtypeStruct((part_lines, width), jnp.float32),
            jax.ShapeDtypeStruct((part_rows, width), jnp.bfloat16),
        ],
        input_output_aliases={4: 0} if given else {},
    )(own, other, table, accum, *given)


def on_device(owners, local_rows, grad_pooled, table, accum, parity, parity_slot):
    table_count = lax.axis_size("table")
    dp_count = lax.axis_size("dp")
    chip_count = table_count // 2
    bag_count = owners.shape[0]
    row_count, row_width = table.shape
    parity_count = parity.shape[0]
    core = lax.axis_index("table") % 2
    dp_index = lax.axis_index("dp")
    pairs = [(i, i ^ 1) for i in range(table_count)]
    same_core = [list(range(c, table_count, 2)) for c in range(2)]

    def swap_cores(values):
        return lax.ppermute(values, "table", pairs)

    def exchange(values):
        return lax.all_to_all(
            values, "table", split_axis=0, concat_axis=0, axis_index_groups=same_core, tiled=True
        )

    half = table_count // 2
    far_grads = lax.ppermute(grad_pooled, "table", [(i, (i + half) % table_count) for i in range(table_count)])
    devices = jnp.arange(table_count, dtype=jnp.int32)[:, None, None]
    requests = jnp.max(jnp.where(owners.T[None] == devices, local_rows.T[None], -1), axis=1)
    asked = exchange(requests.reshape(chip_count, 2, bag_count))
    asked_own = jnp.where(core == 0, asked[:, 0], asked[:, 1])
    asked_other = jnp.where(core == 0, asked[:, 1], asked[:, 0])
    asked_by_peer = swap_cores(asked_other)
    table_half = table.astype(jnp.bfloat16)
    peer_half = swap_cores(table_half)

    part_count = parity_count // dp_count

    def target_of(slot):
        holder, offset = slot // parity_count, slot % parity_count
        mine = (holder % 2 == core) & (offset // part_count == dp_index)
        target = jnp.where(mine, holder // 2 * part_count + offset % part_count, -1)
        return target.reshape(PARTS, -1, 4 * row_width)

    own_target = target_of(parity_slot)
    peer_target = target_of(swap_cores(parity_slot))

    fetched = gather_pair_sums(asked_own, asked_other, table_half, peer_half)

    upper = lax.axis_index("table") >= half
    two_grads = jnp.where(
        upper, jnp.stack([far_grads, grad_pooled]), jnp.stack([grad_pooled, far_grads])
    )
    near = [list(range(h + c, h + half, 2)) for h in (0, half) for c in range(2)]
    own_grads = lax.all_to_all(
        jnp.broadcast_to(two_grads[None], (chip_count // 2,) + two_grads.shape),
        "table", split_axis=0, concat_axis=0, axis_index_groups=near, tiled=True,
    )

    def in_source_order(index):
        index = index.reshape(2, chip_count // 2, bag_count)
        return jnp.swapaxes(index, 0, 1).reshape(chip_count, bag_count)

    named_own, named_by_peer = in_source_order(asked_own), in_source_order(asked_by_peer)
    peer_grads = swap_cores(own_grads)
    grads = [own_grads.reshape(-1, row_width), peer_grads.reshape(-1, row_width)]
    part_rows = row_count // PARTS
    halves = []
    for part in range(PARTS):
        mine = segment_sums(
            [named_own, named_by_peer], grads, part * part_rows, part_rows, jnp.bfloat16
        ).reshape(part_rows, row_width)
        distance = 1
        other = lax.ppermute(mine, "dp", [(i, i ^ 1) for i in range(dp_count)])
        while 2 * distance < dp_count:
            distance *= 2
            mine = (mine.astype(jnp.float32) + other.astype(jnp.float32)).astype(jnp.bfloat16)
            other = lax.ppermute(mine, "dp", [(i, i ^ distance) for i in range(dp_count)])
        halves.append((mine, other))

    returned = exchange(fetched.reshape(chip_count, bag_count, row_width))

    new_table, accums, changes = None, [], None
    accum_lines = accum.reshape(-1, row_width)
    for part, (mine, other) in enumerate(halves):
        new_table, part_accum, delta = update(mine, other, table, accum_lines, part, new_table)
        accums.append(part_accum)
        peer_delta = swap_cores(delta)
        changes = segment_sums(
            [own_target[part], peer_target[part]],
            [delta, peer_delta],
            0,
            chip_count * part_count,
            jnp.bfloat16 if part == PARTS - 1 else jnp.float32,
            changes,
        )
    new_accum = jnp.concatenate(accums, axis=0).reshape(row_count)

    arrived = exchange(changes.reshape(chip_count, part_count, row_width))
    pooled = jnp.sum(returned.astype(jnp.float32), axis=0).astype(jnp.bfloat16)
    part = jnp.sum(arrived.astype(jnp.float32), axis=0).astype(jnp.bfloat16)
    if dp_count == 2:
        other = lax.ppermute(part, "dp", [(0, 1), (1, 0)])
        parts = jnp.where(dp_index == 0, jnp.stack([part, other]), jnp.stack([other, part]))
    else:
        parts = lax.all_gather(part, "dp", axis=0)
    new_parity = parity + parts.reshape(parity_count, row_width).astype(jnp.float32)
    return (pooled, new_table, new_accum, new_parity)


def solution(mesh):
    in_specs = (
        P(("table", "dp"), None),
        P(("table", "dp"), None),
        P(("table", "dp"), None),
        P("table", None),
        P("table"),
        P("table", None),
        P("table"),
    )
    out_specs = (P(("table", "dp"), None), P("table", None), P("table"), P("table", None))

    return jax.shard_map(on_device, mesh=mesh, in_specs=in_specs, out_specs=out_specs, check_vma=False)
```

```python
import functools
import jax
import jax.numpy as jnp
from jax import lax
from jax.experimental import pallas as pl
from jax.experimental.pallas import tpu as pltpu
from jax.sharding import PartitionSpec as P

LEARN = 0.5
EPSILON = 1e-06
SPLIT = 4
PARTS = 2
TABLE_ROWS = 512
NEAR_BYTES = 1 << 21
VMEM = pl.BlockSpec(memory_space=pltpu.VMEM)
SMEM = pl.BlockSpec(memory_space=pltpu.SMEM)


def near(values, copies=1):
    if copies * values.size * values.dtype.itemsize > NEAR_BYTES:
        return values
    return pltpu.with_memory_space_constraint(values, pltpu.MemorySpace.VMEM)


def column_of(row, lanes):
    return jnp.broadcast_to(row, (lanes, row.shape[1])).T


def bits_of(count):
    assert count & (count - 1) == 0
    return count.bit_length() - 1


def split_index(index, low_count):
    return lax.shift_right_arithmetic(index, bits_of(low_count)), lax.bitwise_and(index, low_count - 1)


def side_of(line, side):
    count = line.shape[1] // 2
    return jnp.where(side == 0, line[:, :count], line[:, count:])


def add_segments(total_ref, index, rows, first):
    low_count, spread_width = total_ref.shape
    width = spread_width // SPLIT
    block, low = split_index(index, low_count)
    low = jnp.where((block < 0) | (block >= SPLIT), -1, low)
    hits = (
        (lax.broadcasted_iota(jnp.int32, (low_count, index.shape[1]), 0) == low)
        .astype(jnp.float32)
        .astype(jnp.bfloat16)
    )
    block_column = column_of(block, width)
    rows = rows.astype(jnp.float32)
    spread = jnp.concatenate(
        [jnp.where(block_column == i, rows, 0.0).astype(jnp.bfloat16) for i in range(SPLIT)], axis=1
    )
    part = jnp.dot(hits, spread, preferred_element_type=jnp.float32)
    if first:
        total_ref[...] = part
    else:
        total_ref[...] += part


def put_segments(out_ref, total_ref):
    low_count, width = total_ref.shape[0], out_ref.shape[1]
    for i in range(SPLIT):
        out_ref[i * low_count : (i + 1) * low_count, :] = total_ref[
            :, i * width : (i + 1) * width
        ].astype(out_ref.dtype)


def segment_kernel(place_ref, asked_ref, peer_asked_ref, *refs, base):
    out_ref, total_ref = refs[-2:]
    count = (len(refs) - 2) // 2
    core, chip = place_ref[0], place_ref[1]
    for k in range(count):
        lines = []
        for ref in (asked_ref, peer_asked_ref):
            for source in (chip ^ k, chip ^ k ^ count):
                lines.append(side_of(ref[source], core))
        index = jnp.concatenate(lines, axis=1) - base
        rows = jnp.concatenate([refs[k][...], refs[count + k][...]], axis=0)
        add_segments(total_ref, index, rows, k == 0)
    put_segments(out_ref, total_ref)


def row_gradients(place, asked, peer_asked, grads, peer_grads, base, row_count):
    width = grads[0].shape[1]
    return pl.pallas_call(
        functools.partial(segment_kernel, base=base),
        in_specs=[SMEM] + [VMEM] * (2 + 2 * len(grads)),
        out_specs=VMEM,
        out_shape=pltpu.VMEM((row_count, width), jnp.bfloat16),
        scratch_shapes=[pltpu.VMEM((row_count // SPLIT, SPLIT * width), jnp.float32)],
    )(place, near(asked), near(peer_asked), *[near(g, 2 * len(grads)) for g in (*grads, *peer_grads)])


def gather_kernel(place_ref, asked_ref, own_ref, peer_ref, out_ref, held_ref, *, together):
    chips = asked_ref.shape[0]
    low_count, width = held_ref.shape[1], out_ref.shape[1]
    bags = out_ref.shape[0] // chips
    core = place_ref[0]
    for i in range(SPLIT):
        at = slice(i * low_count, (i + 1) * low_count)
        held_ref[0, :, i * width : (i + 1) * width] = own_ref[at, :].astype(jnp.bfloat16)
        held_ref[1, :, i * width : (i + 1) * width] = peer_ref[at, :]
    for j in range(0, chips, together):
        total = jnp.zeros((together * bags, width), jnp.float32)
        lane = lax.broadcasted_iota(jnp.int32, total.shape, 1)
        for side in range(2):
            index = jnp.concatenate(
                [side_of(asked_ref[j + i], core ^ side) for i in range(together)], axis=1
            )
            block, low = split_index(column_of(index, width), low_count)
            hits = jnp.concatenate(
                [
                    (lane == low - first).astype(jnp.float32).astype(jnp.bfloat16)
                    for first in range(0, low_count, width)
                ],
                axis=1,
            )
            found = jnp.dot(hits, held_ref[side], preferred_element_type=jnp.float32)
            for i in range(SPLIT):
                total += jnp.where(block == i, found[:, i * width : (i + 1) * width], 0.0)
        out_ref[j * bags : (j + together) * bags, :] = total.astype(out_ref.dtype)


def chip_rows(place, asked, own_rows, peer_rows):
    row_count, width = own_rows.shape
    chips, bags = asked.shape[0], asked.shape[2] // 2
    return pl.pallas_call(
        functools.partial(gather_kernel, together=2),
        in_specs=[SMEM, VMEM, VMEM, VMEM],
        out_specs=VMEM,
        out_shape=jax.ShapeDtypeStruct((chips * bags, width), jnp.bfloat16),
        scratch_shapes=[pltpu.VMEM((2, row_count // SPLIT, SPLIT * width), jnp.bfloat16)],
    )(place, *map(near, (asked, own_rows, peer_rows)))


def update_kernel(
    own_ref, other_ref, table_ref, accum_ref, new_table_ref, new_accum_ref, delta_ref, old_ref, sems, *, base
):
    rows, width = own_ref.shape
    copies = [
        pltpu.make_async_copy(
            table_ref.at[pl.ds(base + i * TABLE_ROWS, TABLE_ROWS), :],
            old_ref.at[pl.ds(i * TABLE_ROWS, TABLE_ROWS), :],
            sems.at[i],
        )
        for i in range(rows // TABLE_ROWS)
    ]
    for copy in copies:
        copy.start()
    diagonal = lax.broadcasted_iota(jnp.int32, (width, width), 0) == lax.broadcasted_iota(
        jnp.int32, (width, width), 1
    )
    for j in range(rows // width):
        if j * width % TABLE_ROWS == 0:
            copies[j * width // TABLE_ROWS].wait()
        at = slice(j * width, (j + 1) * width)
        line = base // width + j
        grads = own_ref[at, :].astype(jnp.float32) + other_ref[at, :].astype(jnp.float32)
        scaled = jnp.where(diagonal, accum_ref[line : line + 1, :] * width, 0.0)
        fresh_accum = jnp.sum(grads * grads + scaled, axis=1, keepdims=True) * (1.0 / width)
        old_rows = old_ref[at, :]
        fresh_rows = old_rows - LEARN * grads / jnp.sqrt(fresh_accum + EPSILON)
        new_table_ref[at, :] = fresh_rows
        delta_ref[at, :] = (fresh_rows - old_rows).astype(jnp.bfloat16)
        new_accum_ref[j : j + 1, :] = jnp.sum(
            jnp.where(diagonal, fresh_accum, 0.0), axis=0, keepdims=True
        )


def update(own, other, table, accum, base):
    rows, width = own.shape
    return pl.pallas_call(
        functools.partial(update_kernel, base=base),
        in_specs=[VMEM, VMEM, pl.BlockSpec(memory_space=pl.ANY), VMEM],
        out_specs=[VMEM] * 3,
        out_shape=[
            jax.ShapeDtypeStruct((rows, width), jnp.float32),
            jax.ShapeDtypeStruct((rows // width, width), jnp.float32),
            pltpu.VMEM((rows, width), jnp.bfloat16),
        ],
        scratch_shapes=[
            pltpu.VMEM((rows, width), jnp.float32),
            pltpu.SemaphoreType.DMA((rows // TABLE_ROWS,)),
        ],
    )(near(own), near(other), table, near(accum))


def parity_kernel(place_ref, slot_ref, peer_slot_ref, delta_ref, peer_delta_ref, *refs, base, holder_rows, dp_count, tile):
    start_refs, (out_ref, total_ref) = refs[:-2], refs[-2:]
    core, dp_index = place_ref[0], place_ref[2]
    part_count = holder_rows // dp_count
    line_width = slot_ref.shape[1]
    for k in range(delta_ref.shape[0] // tile):
        first = (base + k * tile) // line_width
        slot = jnp.concatenate(
            [
                ref[first + i : first + i + 1, :]
                for ref in (slot_ref, peer_slot_ref)
                for i in range(tile // line_width)
            ],
            axis=1,
        )
        holder, offset = split_index(slot, holder_rows)
        part, offset = split_index(offset, part_count)
        mine = (lax.bitwise_and(holder, 1) == core) & (part == dp_index)
        target = lax.shift_right_arithmetic(holder, 1) * part_count + offset
        at = slice(k * tile, (k + 1) * tile)
        rows = jnp.concatenate([delta_ref[at, :], peer_delta_ref[at, :]], axis=0)
        add_segments(total_ref, jnp.where(mine, target, -1), rows, k == 0)
    for ref in start_refs:
        total_ref[...] += ref[...]
    if out_ref.shape == total_ref.shape:
        out_ref[...] = total_ref[...]
    else:
        put_segments(out_ref, total_ref)


def parity_changes(place, slot, peer_slot, delta, peer_delta, base, holder_rows, dp_count, segment_count, start, last):
    width = delta.shape[1]
    held = pltpu.VMEM((segment_count // SPLIT, SPLIT * width), jnp.float32)
    return pl.pallas_call(
        functools.partial(
            parity_kernel, base=base, holder_rows=holder_rows, dp_count=dp_count,
            tile=min(1024, delta.shape[0]),
        ),
        in_specs=[SMEM] + [VMEM] * (4 + len(start)),
        out_specs=VMEM,
        out_shape=jax.ShapeDtypeStruct((segment_count, width), jnp.bfloat16) if last else held,
        scratch_shapes=[held],
    )(place, *map(near, (slot, peer_slot, delta, peer_delta, *start)))


def on_device(owners, local_rows, grad_pooled, table, accum, parity, parity_slot):
    table_count = lax.axis_size("table")
    dp_count = lax.axis_size("dp")
    chip_count = table_count // 2
    half = table_count // 2
    bag_count, per_bag = owners.shape
    row_count, width = table.shape
    parity_count = parity.shape[0]
    device = lax.axis_index("table")
    dp_index = lax.axis_index("dp")
    place = jnp.stack([device % 2, device // 2, dp_index]).astype(jnp.int32)
    same_core = [list(range(c, table_count, 2)) for c in range(2)]

    def swap(values, distance):
        return lax.ppermute(values, "table", [(i, i ^ distance) for i in range(table_count)])

    def exchange(values):
        return lax.all_to_all(
            values, "table", split_axis=0, concat_axis=0, axis_index_groups=same_core, tiled=True
        )

    far_grads = swap(grad_pooled, half)

    lanes = jnp.arange(2 * bag_count, dtype=jnp.int32)[None, None, None, :]
    chips = jnp.arange(chip_count, dtype=jnp.int32)[:, None, None, None]
    owners_twice = jnp.tile(owners.T, (1, 2)).reshape(1, 1, per_bag, 2 * bag_count)
    rows_twice = jnp.tile(local_rows.T, (1, 2)).reshape(1, 1, per_bag, 2 * bag_count)
    named = owners_twice == 2 * chips + (lanes >= bag_count).astype(jnp.int32)
    requests = jnp.max(jnp.where(named, rows_twice, -1), axis=2)
    asked = exchange(requests)
    peer_half = swap(table.astype(jnp.bfloat16), 1)
    line_width = 4 * width
    slot_lines = parity_slot.reshape(-1, line_width)
    peer_slot_lines = swap(slot_lines, 1)

    grads = [jnp.concatenate([grad_pooled, far_grads], axis=0)]
    for k in range(1, chip_count // 2):
        grads.append(swap(grads[0], 2 * k))
    peer_asked = swap(asked, 1)
    peer_grads = []
    for values in grads:
        peer_grads.append(swap(values, 1))

    fetched = chip_rows(place, asked, table, peer_half)

    part_rows = row_count // PARTS
    halves = []
    for part in range(PARTS):
        mine = row_gradients(place, asked, peer_asked, grads, peer_grads, part * part_rows, part_rows)
        distance = 1
        other = lax.ppermute(mine, "dp", [(i, i ^ 1) for i in range(dp_count)])
        while 2 * distance < dp_count:
            distance *= 2
            mine = (mine.astype(jnp.float32) + other.astype(jnp.float32)).astype(jnp.bfloat16)
            other = lax.ppermute(mine, "dp", [(i, i ^ distance) for i in range(dp_count)])
        halves.append((mine, other))

    returned = exchange(fetched.reshape(chip_count, bag_count, width))

    part_count = parity_count // dp_count
    tables, accums, changes = [], [], []
    accum_lines = accum.reshape(-1, width)
    for part, (mine, other) in enumerate(halves):
        fresh, fresh_accum, delta = update(mine, other, table, accum_lines, part * part_rows)
        tables.append(fresh)
        accums.append(fresh_accum)
        peer_delta = swap(delta, 1)
        changes = [
            parity_changes(
                place, slot_lines, peer_slot_lines, delta, peer_delta, part * part_rows,
                parity_count, dp_count, chip_count * part_count, changes, part == PARTS - 1,
            )
        ]
    arrived = exchange(changes[0].reshape(chip_count, part_count, width))
    pooled = jnp.sum(returned.astype(jnp.float32), axis=0).astype(jnp.bfloat16)
    new_table = jnp.concatenate(tables, axis=0)
    new_accum = jnp.concatenate(accums, axis=0).reshape(row_count)
    part = jnp.sum(arrived.astype(jnp.float32), axis=0).astype(jnp.bfloat16)
    if dp_count == 2:
        other = lax.ppermute(part, "dp", [(0, 1), (1, 0)])
        parts = jnp.where(dp_index == 0, jnp.stack([part, other]), jnp.stack([other, part]))
    else:
        parts = lax.all_gather(part, "dp", axis=0)
    new_parity = parity + parts.reshape(parity_count, width).astype(jnp.float32)
    return (pooled, new_table, new_accum, new_parity)


def solution(mesh):
    in_specs = (
        P(("table", "dp"), None),
        P(("table", "dp"), None),
        P(("table", "dp"), None),
        P("table", None),
        P("table"),
        P("table", None),
        P("table"),
    )
    out_specs = (P(("table", "dp"), None), P("table", None), P("table"), P("table", None))

    return jax.shard_map(on_device, mesh=mesh, in_specs=in_specs, out_specs=out_specs, check_vma=False)
```

```python
import functools
import jax
import jax.numpy as jnp
from jax import lax
from jax.experimental import pallas as pl
from jax.experimental.pallas import tpu as pltpu
from jax.sharding import PartitionSpec as P

LEARN = 0.5
EPSILON = 1e-06
SPLIT = 4
PARTS = (2, 2)
NEAR_BYTES = 1 << 21
VMEM = pl.BlockSpec(memory_space=pltpu.VMEM)


def near(values, copies=1):
    if copies * values.size * values.dtype.itemsize > NEAR_BYTES:
        return values
    return pltpu.with_memory_space_constraint(values, pltpu.MemorySpace.VMEM)


def column_of(row, lanes):
    return jnp.broadcast_to(row, (lanes, row.shape[1])).T


def bits_of(count):
    assert count & (count - 1) == 0
    return count.bit_length() - 1


def split_index(index, low_count):
    return lax.shift_right_arithmetic(index, bits_of(low_count)), lax.bitwise_and(index, low_count - 1)


def position():
    device = lax.axis_index("table")
    return lax.bitwise_and(device, 1), lax.shift_right_logical(device, 1), lax.axis_index("dp")


def side_of(line, side):
    count = line.shape[1] // 2
    return jnp.where(side == 0, line[:, :count], line[:, count:])


def add_segments(total_ref, index, rows, first):
    low_count, spread_width = total_ref.shape
    width = rows.shape[1]
    split = spread_width // width
    block, low = split_index(index, low_count)
    low = jnp.where((block < 0) | (block >= split), -1, low)
    hits = (
        (lax.broadcasted_iota(jnp.int32, (low_count, index.shape[1]), 0) == low)
        .astype(jnp.float32)
        .astype(jnp.bfloat16)
    )
    block_column = column_of(block, width)
    rows = rows.astype(jnp.float32)
    spread = jnp.concatenate(
        [jnp.where(block_column == i, rows, 0.0).astype(jnp.bfloat16) for i in range(split)], axis=1
    )
    part = jnp.dot(hits, spread, preferred_element_type=jnp.float32)
    if first:
        total_ref[...] = part
    else:
        total_ref[...] += part


def put_segments(out_ref, total_ref):
    low_count, width = total_ref.shape[0], out_ref.shape[1]
    for i in range(total_ref.shape[1] // width):
        out_ref[i * low_count : (i + 1) * low_count, :] = total_ref[
            :, i * width : (i + 1) * width
        ].astype(out_ref.dtype)


def segment_kernel(asked_ref, peer_asked_ref, *refs, base):
    out_ref, total_ref = refs[-2:]
    count = (len(refs) - 2) // 2
    core, chip, _ = position()
    for k in range(count):
        lines = []
        for ref in (asked_ref, peer_asked_ref):
            for source in (chip ^ k, chip ^ k ^ count):
                lines.append(side_of(ref[source], core))
        index = jnp.concatenate(lines, axis=1) - base
        rows = jnp.concatenate([refs[k][...], refs[count + k][...]], axis=0)
        add_segments(total_ref, index, rows, k == 0)
    put_segments(out_ref, total_ref)


def row_gradients(asked, peer_asked, grads, peer_grads, base, row_count):
    width = grads[0].shape[1]
    split = SPLIT if row_count > 4 * 256 else SPLIT // 2
    return pl.pallas_call(
        functools.partial(segment_kernel, base=base),
        in_specs=[VMEM] * (2 + 2 * len(grads)),
        out_specs=VMEM,
        out_shape=pltpu.VMEM((row_count, width), jnp.bfloat16),
        scratch_shapes=[pltpu.VMEM((row_count // split, split * width), jnp.float32)],
    )(near(asked), near(peer_asked), *[near(g, 2 * len(grads)) for g in (*grads, *peer_grads)])


def round_kernel(rows_ref, out_ref, held_ref, sems):
    chunk = rows_ref.shape[0] // SPLIT
    copies = []
    for i in range(SPLIT):
        at = pl.ds(i * chunk, chunk)
        copies.append(pltpu.make_async_copy(rows_ref.at[at, :], held_ref.at[at, :], sems.at[i]))
        copies[i].start()
    for i in range(SPLIT):
        copies[i].wait()
        at = slice(i * chunk, (i + 1) * chunk)
        out_ref[at, :] = held_ref[at, :].astype(jnp.bfloat16)


def rounded(table):
    return pl.pallas_call(
        round_kernel,
        in_specs=[pl.BlockSpec(memory_space=pl.ANY)],
        out_specs=VMEM,
        out_shape=jax.ShapeDtypeStruct(table.shape, jnp.bfloat16),
        scratch_shapes=[pltpu.VMEM(table.shape, table.dtype), pltpu.SemaphoreType.DMA((SPLIT,))],
    )(table)


def gather_kernel(asked_ref, own_ref, peer_ref, out_ref, held_ref, *, together):
    chips = asked_ref.shape[0]
    low_count, width = held_ref.shape[1], out_ref.shape[1]
    bags = out_ref.shape[0] // chips
    core, _, _ = position()
    for i in range(SPLIT):
        at = slice(i * low_count, (i + 1) * low_count)
        held_ref[0, :, i * width : (i + 1) * width] = own_ref[at, :]
        held_ref[1, :, i * width : (i + 1) * width] = peer_ref[at, :]
    for j in range(0, chips, together):
        total = jnp.zeros((together * bags, width), jnp.float32)
        lane = lax.broadcasted_iota(jnp.int32, total.shape, 1)
        for side in range(2):
            index = jnp.concatenate(
                [side_of(asked_ref[j + i], core ^ side) for i in range(together)], axis=1
            )
            block, low = split_index(column_of(index, width), low_count)
            hits = jnp.concatenate(
                [
                    (lane == low - first).astype(jnp.float32).astype(jnp.bfloat16)
                    for first in range(0, low_count, width)
                ],
                axis=1,
            )
            found = jnp.dot(hits, held_ref[side], preferred_element_type=jnp.float32)
            for i in range(SPLIT):
                total += jnp.where(block == i, found[:, i * width : (i + 1) * width], 0.0)
        out_ref[j * bags : (j + together) * bags, :] = total.astype(out_ref.dtype)


def chip_rows(asked, own_rows, peer_rows):
    row_count, width = own_rows.shape
    chips, bags = asked.shape[0], asked.shape[2] // 2
    return pl.pallas_call(
        functools.partial(gather_kernel, together=2),
        in_specs=[VMEM, VMEM, VMEM],
        out_specs=VMEM,
        out_shape=jax.ShapeDtypeStruct((chips * bags, width), jnp.bfloat16),
        scratch_shapes=[pltpu.VMEM((2, row_count // SPLIT, SPLIT * width), jnp.bfloat16)],
    )(near(asked), own_rows, near(peer_rows))


def update_kernel(own_ref, other_ref, table_ref, accum_ref, *refs, base, chunk):
    new_table_ref, new_accum_ref, delta_ref, old_ref, fresh_ref, in_sems, out_sems = refs[-7:]
    rows, width = own_ref.shape
    loads, stores = [], []
    for i in range(rows // chunk):
        here, there = pl.ds(i * chunk, chunk), pl.ds(base + i * chunk, chunk)
        loads.append(pltpu.make_async_copy(table_ref.at[there, :], old_ref.at[here, :], in_sems.at[i]))
        stores.append(
            pltpu.make_async_copy(fresh_ref.at[here, :], new_table_ref.at[there, :], out_sems.at[i])
        )
    for copy in loads:
        copy.start()
    diagonal = lax.broadcasted_iota(jnp.int32, (width, width), 0) == lax.broadcasted_iota(
        jnp.int32, (width, width), 1
    )
    for j in range(rows // width):
        i, within = divmod(j * width, chunk)
        if within == 0:
            loads[i].wait()
        at = slice(j * width, (j + 1) * width)
        line = base // width + j
        grads = own_ref[at, :].astype(jnp.float32) + other_ref[at, :].astype(jnp.float32)
        scaled = jnp.where(diagonal, accum_ref[line : line + 1, :] * width, 0.0)
        fresh_accum = jnp.sum(grads * grads + scaled, axis=1, keepdims=True) * (1.0 / width)
        old_rows = old_ref[at, :]
        fresh_rows = old_rows - LEARN * grads / jnp.sqrt(fresh_accum + EPSILON)
        fresh_ref[at, :] = fresh_rows
        if within + width == chunk:
            stores[i].start()
        delta_ref[at, :] = (fresh_rows - old_rows).astype(jnp.bfloat16)
        new_accum_ref[j : j + 1, :] = jnp.sum(
            jnp.where(diagonal, fresh_accum, 0.0), axis=0, keepdims=True
        )
    for copy in stores:
        copy.wait()


def update(own, other, table, accum, base, unfinished):
    rows, width = own.shape
    chunk = min(256, rows)
    anywhere = pl.BlockSpec(memory_space=pl.ANY)
    return pl.pallas_call(
        functools.partial(update_kernel, base=base, chunk=chunk),
        in_specs=[VMEM, VMEM, anywhere, VMEM] + [anywhere] * len(unfinished),
        out_specs=[anywhere, VMEM, VMEM],
        out_shape=[
            jax.ShapeDtypeStruct(table.shape, jnp.float32),
            jax.ShapeDtypeStruct((rows // width, width), jnp.float32),
            pltpu.VMEM((rows, width), jnp.bfloat16),
        ],
        scratch_shapes=[
            pltpu.VMEM((rows, width), jnp.float32),
            pltpu.VMEM((rows, width), jnp.float32),
            pltpu.SemaphoreType.DMA((rows // chunk,)),
            pltpu.SemaphoreType.DMA((rows // chunk,)),
        ],
        input_output_aliases={4: 0} if unfinished else {},
    )(near(own), near(other), table, near(accum), *unfinished)


def parity_kernel(slot_ref, peer_slot_ref, delta_ref, peer_delta_ref, *refs, base, holder_rows, dp_count, tile, last):
    refs, total_ref = refs[:-1], refs[-1]
    if base > 0:
        start_ref, refs, held_ref, sem = refs[0], refs[1:-2], refs[-2], refs[-1]
        copy = pltpu.make_async_copy(start_ref, held_ref, sem)
        copy.start()
    core, chip, dp_index = position()
    part_count = holder_rows // dp_count
    line_width = slot_ref.shape[1]
    width = delta_ref.shape[1]
    for k in range(delta_ref.shape[0] // tile):
        first = (base + k * tile) // line_width
        slot = jnp.concatenate(
            [
                ref[first + i : first + i + 1, :]
                for ref in (slot_ref, peer_slot_ref)
                for i in range(tile // line_width)
            ],
            axis=1,
        )
        holder, offset = split_index(slot, holder_rows)
        part, offset = split_index(offset, part_count)
        mine = (lax.bitwise_and(holder, 1) == core) & (part == dp_index)
        target = lax.bitwise_xor(lax.shift_right_arithmetic(holder, 1), chip) * part_count + offset
        at = slice(k * tile, (k + 1) * tile)
        rows = jnp.concatenate([delta_ref[at, :], peer_delta_ref[at, :]], axis=0)
        add_segments(total_ref, jnp.where(mine, target, -1), rows, k == 0)
    if base > 0:
        copy.wait()
        total_ref[...] += held_ref[...]
    if not last:
        refs[-1][...] = total_ref[...]
        return
    low_count = total_ref.shape[0]
    out_refs = refs[-(low_count * SPLIT // part_count) :]
    for i, out_ref in enumerate(out_refs):
        block, low = divmod(i * part_count, low_count)
        out_ref[...] = total_ref[
            low : low + part_count, block * width : (block + 1) * width
        ].astype(out_ref.dtype)


def parity_changes(slot, peer_slot, delta, peer_delta, base, holder_rows, dp_count, chip_count, start, last):
    width = delta.shape[1]
    part_count = holder_rows // dp_count
    segment_count = chip_count * part_count
    held = pltpu.VMEM((segment_count // SPLIT, SPLIT * width), jnp.float32)
    return pl.pallas_call(
        functools.partial(
            parity_kernel, base=base, holder_rows=holder_rows, dp_count=dp_count,
            tile=min(1024, delta.shape[0]), last=last,
        ),
        in_specs=[VMEM] * 4 + [pl.BlockSpec(memory_space=pl.ANY)] * len(start),
        out_specs=[VMEM] * chip_count if last else VMEM,
        out_shape=[pltpu.VMEM((part_count, width), jnp.bfloat16)] * chip_count
        if last
        else jax.ShapeDtypeStruct(held.shape, held.dtype),
        scratch_shapes=([held, pltpu.SemaphoreType.DMA] if start else []) + [held],
    )(*map(near, (slot, peer_slot, delta, peer_delta)), *start)


def on_device(owners, local_rows, grad_pooled, table, accum, parity, parity_slot):
    table_count = lax.axis_size("table")
    dp_count = lax.axis_size("dp")
    chip_count = table_count // 2
    half = table_count // 2
    bag_count, per_bag = owners.shape
    row_count, width = table.shape
    parity_count = parity.shape[0]
    dp_index = lax.axis_index("dp")
    same_core = [list(range(c, table_count, 2)) for c in range(2)]

    def swap(values, distance):
        return lax.ppermute(values, "table", [(i, i ^ distance) for i in range(table_count)])

    def exchange(values):
        return lax.all_to_all(
            values, "table", split_axis=0, concat_axis=0, axis_index_groups=same_core, tiled=True
        )

    far_grads = swap(grad_pooled, half)

    lanes = jnp.arange(2 * bag_count, dtype=jnp.int32)[None, None, None, :]
    chips = jnp.arange(chip_count, dtype=jnp.int32)[:, None, None, None]
    owners_twice = jnp.tile(owners.T, (1, 2)).reshape(1, 1, per_bag, 2 * bag_count)
    rows_twice = jnp.tile(local_rows.T, (1, 2)).reshape(1, 1, per_bag, 2 * bag_count)
    named = owners_twice == 2 * chips + (lanes >= bag_count).astype(jnp.int32)
    requests = jnp.max(jnp.where(named, rows_twice, -1), axis=2)
    asked = exchange(requests)
    own_table = rounded(table)
    peer_table = swap(own_table, 1)
    line_width = 4 * width
    slot_lines = parity_slot.reshape(-1, line_width)
    peer_slot_lines = swap(slot_lines, 1)

    grads = [jnp.concatenate([grad_pooled, far_grads], axis=0)]
    for k in range(1, chip_count // 2):
        grads.append(swap(grads[0], 2 * k))
    peer_asked = swap(asked, 1)
    peer_grads = []
    for values in grads:
        peer_grads.append(swap(values, 1))

    fetched = chip_rows(asked, own_table, peer_table)

    halves, bases = [], []
    for part, share in enumerate(PARTS):
        part_rows = row_count // share
        bases.append(sum(row_count // other for other in PARTS[:part]))
        mine = row_gradients(asked, peer_asked, grads, peer_grads, bases[part], part_rows)
        distance = 1
        other = lax.ppermute(mine, "dp", [(i, i ^ 1) for i in range(dp_count)])
        while 2 * distance < dp_count:
            distance *= 2
            mine = (mine.astype(jnp.float32) + other.astype(jnp.float32)).astype(jnp.bfloat16)
            other = lax.ppermute(mine, "dp", [(i, i ^ distance) for i in range(dp_count)])
        halves.append((mine, other))

    returned = exchange(fetched.reshape(chip_count, bag_count, width))

    new_table, accums, changes = [], [], []
    accum_lines = accum.reshape(-1, width)
    for part, (mine, other) in enumerate(halves):
        fresh, fresh_accum, delta = update(mine, other, table, accum_lines, bases[part], new_table)
        new_table = [fresh]
        accums.append(fresh_accum)
        peer_delta = swap(delta, 1)
        changes = parity_changes(
            slot_lines, peer_slot_lines, delta, peer_delta, bases[part],
            parity_count, dp_count, chip_count, changes, part == len(PARTS) - 1,
        )
        if part < len(PARTS) - 1:
            changes = [changes]
    arrived = [changes[0]]
    for k in range(1, chip_count):
        arrived.append(swap(changes[k], 2 * k))
    pooled = jnp.sum(returned.astype(jnp.float32), axis=0).astype(jnp.bfloat16)
    new_accum = jnp.concatenate(accums, axis=0).reshape(row_count)
    part = sum(values.astype(jnp.float32) for values in arrived).astype(jnp.bfloat16)
    if dp_count == 2:
        other = lax.ppermute(part, "dp", [(0, 1), (1, 0)])
        parts = jnp.where(dp_index == 0, jnp.stack([part, other]), jnp.stack([other, part]))
    else:
        parts = lax.all_gather(part, "dp", axis=0)
    new_parity = parity + parts.reshape(parity_count, width).astype(jnp.float32)
    return (pooled, new_table[0], new_accum, new_parity)


def solution(mesh):
    in_specs = (
        P(("table", "dp"), None),
        P(("table", "dp"), None),
        P(("table", "dp"), None),
        P("table", None),
        P("table"),
        P("table", None),
        P("table"),
    )
    out_specs = (P(("table", "dp"), None), P("table", None), P("table"), P("table", None))

    return jax.shard_map(on_device, mesh=mesh, in_specs=in_specs, out_specs=out_specs, check_vma=False)
```

```python
import functools
import jax
import jax.numpy as jnp
from jax import lax
from jax.experimental import pallas as pl
from jax.experimental.pallas import tpu as pltpu
from jax.sharding import PartitionSpec as P

LEARN = 0.5
EPSILON = 1e-06
SPLIT = 4
PARTS = (4, 2, 4)
NEAR_BYTES = 1 << 21
VMEM = pl.BlockSpec(memory_space=pltpu.VMEM)


def near(values, copies=1):
    if copies * values.size * values.dtype.itemsize > NEAR_BYTES:
        return values
    return pltpu.with_memory_space_constraint(values, pltpu.MemorySpace.VMEM)


def column_of(row, lanes):
    return jnp.broadcast_to(row, (lanes, row.shape[1])).T


def bits_of(count):
    assert count & (count - 1) == 0
    return count.bit_length() - 1


def split_index(index, low_count):
    return lax.shift_right_arithmetic(index, bits_of(low_count)), lax.bitwise_and(index, low_count - 1)


def position():
    device = lax.axis_index("table")
    return lax.bitwise_and(device, 1), lax.shift_right_logical(device, 1), lax.axis_index("dp")


def side_of(line, side):
    count = line.shape[1] // 2
    return jnp.where(side == 0, line[:, :count], line[:, count:])


def add_segments(total_ref, index, rows, first):
    low_count, spread_width = total_ref.shape
    width = rows.shape[1]
    split = spread_width // width
    block, low = split_index(index, low_count)
    low = jnp.where((block < 0) | (block >= split), -1, low)
    hits = (
        (lax.broadcasted_iota(jnp.int32, (low_count, index.shape[1]), 0) == low)
        .astype(jnp.float32)
        .astype(jnp.bfloat16)
    )
    block_column = column_of(block, width)
    rows = rows.astype(jnp.float32)
    spread = jnp.concatenate(
        [jnp.where(block_column == i, rows, 0.0).astype(jnp.bfloat16) for i in range(split)], axis=1
    )
    part = jnp.dot(hits, spread, preferred_element_type=jnp.float32)
    if first:
        total_ref[...] = part
    else:
        total_ref[...] += part


def put_segments(out_ref, total_ref):
    low_count, width = total_ref.shape[0], out_ref.shape[1]
    for i in range(total_ref.shape[1] // width):
        out_ref[i * low_count : (i + 1) * low_count, :] = total_ref[
            :, i * width : (i + 1) * width
        ].astype(out_ref.dtype)


def segment_kernel(asked_ref, peer_asked_ref, *refs, base):
    out_ref, total_ref = refs[-2:]
    count = (len(refs) - 2) // 2
    core, chip, _ = position()
    for k in range(count):
        lines = []
        for ref in (asked_ref, peer_asked_ref):
            for source in (chip ^ k, chip ^ k ^ count):
                lines.append(side_of(ref[source], core))
        index = jnp.concatenate(lines, axis=1) - base
        rows = jnp.concatenate([refs[k][...], refs[count + k][...]], axis=0)
        add_segments(total_ref, index, rows, k == 0)
    put_segments(out_ref, total_ref)


def row_gradients(asked, peer_asked, grads, peer_grads, base, row_count):
    width = grads[0].shape[1]
    split = SPLIT if row_count > 4 * 256 else SPLIT // 2
    return pl.pallas_call(
        functools.partial(segment_kernel, base=base),
        in_specs=[VMEM] * (2 + 2 * len(grads)),
        out_specs=VMEM,
        out_shape=pltpu.VMEM((row_count, width), jnp.bfloat16),
        scratch_shapes=[pltpu.VMEM((row_count // split, split * width), jnp.float32)],
    )(near(asked), near(peer_asked), *[near(g, 2 * len(grads)) for g in (*grads, *peer_grads)])


def round_kernel(rows_ref, out_ref, held_ref, sems):
    chunk = rows_ref.shape[0] // SPLIT
    copies = []
    for i in range(SPLIT):
        at = pl.ds(i * chunk, chunk)
        copies.append(pltpu.make_async_copy(rows_ref.at[at, :], held_ref.at[at, :], sems.at[i]))
        copies[i].start()
    for i in range(SPLIT):
        copies[i].wait()
        at = slice(i * chunk, (i + 1) * chunk)
        out_ref[at, :] = held_ref[at, :].astype(jnp.bfloat16)


def rounded(table):
    return pl.pallas_call(
        round_kernel,
        in_specs=[pl.BlockSpec(memory_space=pl.ANY)],
        out_specs=VMEM,
        out_shape=jax.ShapeDtypeStruct(table.shape, jnp.bfloat16),
        scratch_shapes=[pltpu.VMEM(table.shape, table.dtype), pltpu.SemaphoreType.DMA((SPLIT,))],
    )(table)


def gather_kernel(asked_ref, own_ref, peer_ref, out_ref, held_ref, *, together):
    chips = asked_ref.shape[0]
    low_count, width = held_ref.shape[1], out_ref.shape[1]
    bags = out_ref.shape[0] // chips
    core, _, _ = position()
    for i in range(SPLIT):
        at = slice(i * low_count, (i + 1) * low_count)
        held_ref[0, :, i * width : (i + 1) * width] = own_ref[at, :]
        held_ref[1, :, i * width : (i + 1) * width] = peer_ref[at, :]
    for j in range(0, chips, together):
        total = jnp.zeros((together * bags, width), jnp.float32)
        lane = lax.broadcasted_iota(jnp.int32, total.shape, 1)
        for side in range(2):
            index = jnp.concatenate(
                [side_of(asked_ref[j + i], core ^ side) for i in range(together)], axis=1
            )
            block, low = split_index(column_of(index, width), low_count)
            hits = jnp.concatenate(
                [
                    (lane == low - first).astype(jnp.float32).astype(jnp.bfloat16)
                    for first in range(0, low_count, width)
                ],
                axis=1,
            )
            found = jnp.dot(hits, held_ref[side], preferred_element_type=jnp.float32)
            for i in range(SPLIT):
                total += jnp.where(block == i, found[:, i * width : (i + 1) * width], 0.0)
        out_ref[j * bags : (j + together) * bags, :] = total.astype(out_ref.dtype)


def chip_rows(asked, own_rows, peer_rows):
    row_count, width = own_rows.shape
    chips, bags = asked.shape[0], asked.shape[2] // 2
    return pl.pallas_call(
        functools.partial(gather_kernel, together=2),
        in_specs=[VMEM, VMEM, VMEM],
        out_specs=VMEM,
        out_shape=jax.ShapeDtypeStruct((chips * bags, width), jnp.bfloat16),
        scratch_shapes=[pltpu.VMEM((2, row_count // SPLIT, SPLIT * width), jnp.bfloat16)],
    )(near(asked), own_rows, near(peer_rows))


def update_kernel(own_ref, other_ref, table_ref, accum_ref, *refs, base, chunk):
    new_table_ref, new_accum_ref, delta_ref, old_ref, fresh_ref, in_sems, out_sems = refs[-7:]
    rows, width = own_ref.shape
    loads, stores = [], []
    for i in range(rows // chunk):
        here, there = pl.ds(i * chunk, chunk), pl.ds(base + i * chunk, chunk)
        loads.append(pltpu.make_async_copy(table_ref.at[there, :], old_ref.at[here, :], in_sems.at[i]))
        stores.append(
            pltpu.make_async_copy(fresh_ref.at[here, :], new_table_ref.at[there, :], out_sems.at[i])
        )
    for copy in loads:
        copy.start()
    diagonal = lax.broadcasted_iota(jnp.int32, (width, width), 0) == lax.broadcasted_iota(
        jnp.int32, (width, width), 1
    )
    ones = jnp.ones((3 * width, width), jnp.bfloat16)
    for j in range(rows // width):
        i, within = divmod(j * width, chunk)
        if within == 0:
            loads[i].wait()
        at = slice(j * width, (j + 1) * width)
        line = base // width + j
        grads = own_ref[at, :].astype(jnp.float32) + other_ref[at, :].astype(jnp.float32)
        scaled = jnp.where(diagonal, accum_ref[line : line + 1, :] * width, 0.0)
        rest, terms = grads * grads + scaled, []
        for _ in range(3):
            terms.append(rest.astype(jnp.bfloat16))
            rest = rest - terms[-1].astype(jnp.float32)
        sums = jnp.dot(jnp.concatenate(terms, axis=1), ones, preferred_element_type=jnp.float32)
        fresh_accum = sums * (1.0 / width)
        old_rows = old_ref[at, :]
        fresh_rows = old_rows - LEARN * grads / jnp.sqrt(fresh_accum + EPSILON)
        fresh_ref[at, :] = fresh_rows
        if within + width == chunk:
            stores[i].start()
        delta_ref[at, :] = (fresh_rows - old_rows).astype(jnp.bfloat16)
        new_accum_ref[j : j + 1, :] = jnp.sum(
            jnp.where(diagonal, fresh_accum, 0.0), axis=0, keepdims=True
        )
    for copy in stores:
        copy.wait()


def update(own, other, table, accum, base, unfinished):
    rows, width = own.shape
    chunk = min(256, rows)
    anywhere = pl.BlockSpec(memory_space=pl.ANY)
    return pl.pallas_call(
        functools.partial(update_kernel, base=base, chunk=chunk),
        in_specs=[VMEM, VMEM, anywhere, VMEM] + [anywhere] * len(unfinished),
        out_specs=[anywhere, VMEM, VMEM],
        out_shape=[
            jax.ShapeDtypeStruct(table.shape, jnp.float32),
            jax.ShapeDtypeStruct((rows // width, width), jnp.float32),
            pltpu.VMEM((rows, width), jnp.bfloat16),
        ],
        scratch_shapes=[
            pltpu.VMEM((rows, width), jnp.float32),
            pltpu.VMEM((rows, width), jnp.float32),
            pltpu.SemaphoreType.DMA((rows // chunk,)),
            pltpu.SemaphoreType.DMA((rows // chunk,)),
        ],
        input_output_aliases={4: 0} if unfinished else {},
    )(near(own), near(other), table, near(accum), *unfinished)


def parity_kernel(slot_ref, peer_slot_ref, delta_ref, peer_delta_ref, *refs, base, holder_rows, dp_count, tile, last):
    refs, total_ref = refs[:-1], refs[-1]
    if base > 0:
        start_ref, refs, held_ref, sem = refs[0], refs[1:-2], refs[-2], refs[-1]
        copy = pltpu.make_async_copy(start_ref, held_ref, sem)
        copy.start()
    core, chip, dp_index = position()
    part_count = holder_rows // dp_count
    line_width = slot_ref.shape[1]
    width = delta_ref.shape[1]
    for k in range(delta_ref.shape[0] // tile):
        first = (base + k * tile) // line_width
        slot = jnp.concatenate(
            [
                ref[first + i : first + i + 1, :]
                for ref in (slot_ref, peer_slot_ref)
                for i in range(tile // line_width)
            ],
            axis=1,
        )
        holder, offset = split_index(slot, holder_rows)
        part, offset = split_index(offset, part_count)
        mine = (lax.bitwise_and(holder, 1) == core) & (part == dp_index)
        target = lax.bitwise_xor(lax.shift_right_arithmetic(holder, 1), chip) * part_count + offset
        at = slice(k * tile, (k + 1) * tile)
        rows = jnp.concatenate([delta_ref[at, :], peer_delta_ref[at, :]], axis=0)
        add_segments(total_ref, jnp.where(mine, target, -1), rows, k == 0)
    if base > 0:
        copy.wait()
        total_ref[...] += held_ref[...]
    if not last:
        refs[-1][...] = total_ref[...]
        return
    low_count = total_ref.shape[0]
    out_refs = refs[-(low_count * SPLIT // part_count) :]
    for i, out_ref in enumerate(out_refs):
        block, low = divmod(i * part_count, low_count)
        out_ref[...] = total_ref[
            low : low + part_count, block * width : (block + 1) * width
        ].astype(out_ref.dtype)


def parity_changes(slot, peer_slot, delta, peer_delta, base, holder_rows, dp_count, chip_count, start, last):
    width = delta.shape[1]
    part_count = holder_rows // dp_count
    segment_count = chip_count * part_count
    held = pltpu.VMEM((segment_count // SPLIT, SPLIT * width), jnp.float32)
    return pl.pallas_call(
        functools.partial(
            parity_kernel, base=base, holder_rows=holder_rows, dp_count=dp_count,
            tile=min(1024, delta.shape[0]), last=last,
        ),
        in_specs=[VMEM] * 4 + [pl.BlockSpec(memory_space=pl.ANY)] * len(start),
        out_specs=[VMEM] * chip_count if last else VMEM,
        out_shape=[pltpu.VMEM((part_count, width), jnp.bfloat16)] * chip_count
        if last
        else jax.ShapeDtypeStruct(held.shape, held.dtype),
        scratch_shapes=([held, pltpu.SemaphoreType.DMA] if start else []) + [held],
    )(*map(near, (slot, peer_slot, delta, peer_delta)), *start)


def on_device(owners, local_rows, grad_pooled, table, accum, parity, parity_slot):
    table_count = lax.axis_size("table")
    dp_count = lax.axis_size("dp")
    chip_count = table_count // 2
    half = table_count // 2
    bag_count, per_bag = owners.shape
    row_count, width = table.shape
    parity_count = parity.shape[0]
    dp_index = lax.axis_index("dp")
    same_core = [list(range(c, table_count, 2)) for c in range(2)]

    def swap(values, distance):
        return lax.ppermute(values, "table", [(i, i ^ distance) for i in range(table_count)])

    def exchange(values):
        return lax.all_to_all(
            values, "table", split_axis=0, concat_axis=0, axis_index_groups=same_core, tiled=True
        )

    far_grads = swap(grad_pooled, half)

    lanes = jnp.arange(2 * bag_count, dtype=jnp.int32)[None, None, None, :]
    chips = jnp.arange(chip_count, dtype=jnp.int32)[:, None, None, None]
    owners_twice = jnp.tile(owners.T, (1, 2)).reshape(1, 1, per_bag, 2 * bag_count)
    rows_twice = jnp.tile(local_rows.T, (1, 2)).reshape(1, 1, per_bag, 2 * bag_count)
    named = owners_twice == 2 * chips + (lanes >= bag_count).astype(jnp.int32)
    requests = jnp.max(jnp.where(named, rows_twice, -1), axis=2)
    asked = exchange(requests)
    own_table = rounded(table)
    peer_table = swap(own_table, 1)
    line_width = 4 * width
    slot_lines = parity_slot.reshape(-1, line_width)
    peer_slot_lines = swap(slot_lines, 1)

    grads = [jnp.concatenate([grad_pooled, far_grads], axis=0)]
    for k in range(1, chip_count // 2):
        grads.append(swap(grads[0], 2 * k))
    peer_asked = swap(asked, 1)
    peer_grads = []
    for values in grads:
        peer_grads.append(swap(values, 1))

    fetched = chip_rows(asked, own_table, peer_table)

    halves, bases = [], []
    for part, share in enumerate(PARTS):
        part_rows = row_count // share
        bases.append(sum(row_count // other for other in PARTS[:part]))
        mine = row_gradients(asked, peer_asked, grads, peer_grads, bases[part], part_rows)
        distance = 1
        other = lax.ppermute(mine, "dp", [(i, i ^ 1) for i in range(dp_count)])
        while 2 * distance < dp_count:
            distance *= 2
            mine = (mine.astype(jnp.float32) + other.astype(jnp.float32)).astype(jnp.bfloat16)
            other = lax.ppermute(mine, "dp", [(i, i ^ distance) for i in range(dp_count)])
        halves.append((mine, other))

    returned = exchange(fetched.reshape(chip_count, bag_count, width))

    new_table, accums, changes = [], [], []
    accum_lines = accum.reshape(-1, width)
    for part, (mine, other) in enumerate(halves):
        fresh, fresh_accum, delta = update(mine, other, table, accum_lines, bases[part], new_table)
        new_table = [fresh]
        accums.append(fresh_accum)
        peer_delta = swap(delta, 1)
        changes = parity_changes(
            slot_lines, peer_slot_lines, delta, peer_delta, bases[part],
            parity_count, dp_count, chip_count, changes, part == len(PARTS) - 1,
        )
        if part < len(PARTS) - 1:
            changes = [changes]
    arrived = [changes[0]]
    for k in range(1, chip_count):
        arrived.append(swap(changes[k], 2 * k))
    pooled = jnp.sum(returned.astype(jnp.float32), axis=0).astype(jnp.bfloat16)
    new_accum = jnp.concatenate(accums, axis=0).reshape(row_count)
    part = sum(values.astype(jnp.float32) for values in arrived).astype(jnp.bfloat16)
    if dp_count == 2:
        other = lax.ppermute(part, "dp", [(0, 1), (1, 0)])
        parts = jnp.where(dp_index == 0, jnp.stack([part, other]), jnp.stack([other, part]))
    else:
        parts = lax.all_gather(part, "dp", axis=0)
    new_parity = parity + parts.reshape(parity_count, width).astype(jnp.float32)
    return (pooled, new_table[0], new_accum, new_parity)


def solution(mesh):
    in_specs = (
        P(("table", "dp"), None),
        P(("table", "dp"), None),
        P(("table", "dp"), None),
        P("table", None),
        P("table"),
        P("table", None),
        P("table"),
    )
    out_specs = (P(("table", "dp"), None), P("table", None), P("table"), P("table", None))

    return jax.shard_map(on_device, mesh=mesh, in_specs=in_specs, out_specs=out_specs, check_vma=False)
```

```python
import functools
import jax
import jax.numpy as jnp
from jax import lax
from jax.experimental import pallas as pl
from jax.experimental.pallas import tpu as pltpu
from jax.sharding import PartitionSpec as P

LEARN = 0.5
EPSILON = 1e-06
SPLIT = 4
PARTS = (2, 2)
NEAR_BYTES = 1 << 21
VMEM = pl.BlockSpec(memory_space=pltpu.VMEM)


def near(values, copies=1):
    if copies * values.size * values.dtype.itemsize > NEAR_BYTES:
        return values
    return pltpu.with_memory_space_constraint(values, pltpu.MemorySpace.VMEM)


def column_of(row, lanes):
    return jnp.broadcast_to(row, (lanes, row.shape[1])).T


def bits_of(count):
    assert count & (count - 1) == 0
    return count.bit_length() - 1


def split_index(index, low_count):
    return lax.shift_right_arithmetic(index, bits_of(low_count)), lax.bitwise_and(index, low_count - 1)


def position():
    device = lax.axis_index("table")
    return lax.bitwise_and(device, 1), lax.shift_right_logical(device, 1), lax.axis_index("dp")


def add_segments(total_ref, index, rows, first):
    low_count, spread_width = total_ref.shape
    width = rows.shape[1]
    split = spread_width // width
    block, low = split_index(index, low_count)
    low = jnp.where((block < 0) | (block >= split), -1, low)
    hits = (
        (lax.broadcasted_iota(jnp.int32, (low_count, index.shape[1]), 0) == low)
        .astype(jnp.float32)
        .astype(jnp.bfloat16)
    )
    block_column = column_of(block, width)
    rows = rows.astype(jnp.float32)
    spread = jnp.concatenate(
        [jnp.where(block_column == i, rows, 0.0).astype(jnp.bfloat16) for i in range(split)], axis=1
    )
    part = jnp.dot(hits, spread, preferred_element_type=jnp.float32)
    if first:
        total_ref[...] = part
    else:
        total_ref[...] += part


def put_segments(out_ref, total_ref):
    low_count, width = total_ref.shape[0], out_ref.shape[1]
    for i in range(total_ref.shape[1] // width):
        out_ref[i * low_count : (i + 1) * low_count, :] = total_ref[
            :, i * width : (i + 1) * width
        ].astype(out_ref.dtype)


def segment_kernel(asked_ref, *refs, base):
    out_ref, total_ref = refs[-2:]
    count = (len(refs) - 2) // 2
    core, chip, _ = position()
    for k in range(count):
        sources = [2 * (chip ^ k ^ far) + (core ^ side) for side in range(2) for far in (0, count)]
        index = jnp.concatenate([asked_ref[source] for source in sources], axis=1) - base
        rows = jnp.concatenate([refs[k][...], refs[count + k][...]], axis=0)
        add_segments(total_ref, index, rows, k == 0)
    put_segments(out_ref, total_ref)


def row_gradients(asked, grads, peer_grads, base, row_count):
    width = grads[0].shape[1]
    split = SPLIT if row_count > 4 * 256 else SPLIT // 2
    return pl.pallas_call(
        functools.partial(segment_kernel, base=base),
        in_specs=[VMEM] * (1 + 2 * len(grads)),
        out_specs=VMEM,
        out_shape=pltpu.VMEM((row_count, width), jnp.bfloat16),
        scratch_shapes=[pltpu.VMEM((row_count // split, split * width), jnp.float32)],
    )(near(asked), *[near(g, 2 * len(grads)) for g in (*grads, *peer_grads)])


def gather_kernel(asked_ref, table_ref, *refs, together):
    out_refs, (arrived_ref, held_ref, sems) = refs[:2], refs[2:]
    low_count, width = held_ref.shape[0], table_ref.shape[1]
    bags = asked_ref.shape[2]
    core, _, _ = position()
    copies = []
    for i in range(SPLIT):
        at = pl.ds(i * low_count, low_count)
        copies.append(pltpu.make_async_copy(table_ref.at[at, :], arrived_ref.at[at, :], sems.at[i]))
        copies[i].start()
    for i in range(SPLIT):
        copies[i].wait()
        rows = arrived_ref[i * low_count : (i + 1) * low_count, :]
        held_ref[:, i * width : (i + 1) * width] = rows.astype(jnp.bfloat16)
    lane = lax.broadcasted_iota(jnp.int32, (together * bags, width), 1)
    for side in (1, 0):
        for j in range(0, asked_ref.shape[0] // 2, together):
            index = jnp.concatenate(
                [asked_ref[2 * (j + i) + (core ^ side)] for i in range(together)], axis=1
            )
            block, low = split_index(column_of(index, width), low_count)
            hits = jnp.concatenate(
                [
                    (lane == low - first).astype(jnp.float32).astype(jnp.bfloat16)
                    for first in range(0, low_count, width)
                ],
                axis=1,
            )
            found = jnp.dot(hits, held_ref[...], preferred_element_type=jnp.float32)
            row = jnp.where(block == 0, found[:, :width], 0.0)
            for i in range(1, SPLIT):
                row = jnp.where(block == i, found[:, i * width : (i + 1) * width], row)
            out_refs[side][j * bags : (j + together) * bags, :] = row.astype(jnp.bfloat16)


def named_rows(asked, table):
    row_count, width = table.shape
    sources, _, bags = asked.shape
    rows = jax.ShapeDtypeStruct((sources // 2 * bags, width), jnp.bfloat16)
    return pl.pallas_call(
        functools.partial(gather_kernel, together=2),
        in_specs=[VMEM, pl.BlockSpec(memory_space=pl.ANY)],
        out_specs=[VMEM, VMEM],
        out_shape=[rows, rows],
        scratch_shapes=[
            pltpu.VMEM(table.shape, table.dtype),
            pltpu.VMEM((row_count // SPLIT, SPLIT * width), jnp.bfloat16),
            pltpu.SemaphoreType.DMA((SPLIT,)),
        ],
    )(near(asked), table)


def diagonal_of(width):
    rows = lax.broadcasted_iota(jnp.int32, (width, width), 0)
    return rows == lax.broadcasted_iota(jnp.int32, (width, width), 1)


def fresh_accum_of(grads, accum_line, diagonal):
    width = grads.shape[1]
    rest, terms = grads * grads + jnp.where(diagonal, accum_line * width, 0.0), []
    for _ in range(3):
        terms.append(rest.astype(jnp.bfloat16))
        rest = rest - terms[-1].astype(jnp.float32)
    ones = jnp.ones((3 * width, width), jnp.bfloat16)
    sums = jnp.dot(jnp.concatenate(terms, axis=1), ones, preferred_element_type=jnp.float32)
    return sums * (1.0 / width)


def change_kernel(own_ref, other_ref, accum_ref, new_accum_ref, delta_ref, *, base):
    rows, width = own_ref.shape
    diagonal = diagonal_of(width)
    for j in range(rows // width):
        at = slice(j * width, (j + 1) * width)
        line = base // width + j
        grads = own_ref[at, :].astype(jnp.float32) + other_ref[at, :].astype(jnp.float32)
        fresh_accum = fresh_accum_of(grads, accum_ref[line : line + 1, :], diagonal)
        delta_ref[at, :] = (-LEARN * grads / jnp.sqrt(fresh_accum + EPSILON)).astype(jnp.bfloat16)
        new_accum_ref[j : j + 1, :] = jnp.sum(
            jnp.where(diagonal, fresh_accum, 0.0), axis=0, keepdims=True
        )


def changes_of(own, other, accum, base):
    rows, width = own.shape
    return pl.pallas_call(
        functools.partial(change_kernel, base=base),
        in_specs=[VMEM] * 3,
        out_specs=[VMEM, VMEM],
        out_shape=[
            jax.ShapeDtypeStruct((rows // width, width), jnp.float32),
            pltpu.VMEM((rows, width), jnp.bfloat16),
        ],
    )(*map(near, (own, other, accum)))


def finish_kernel(*refs, parts):
    accum_ref, table_ref, out_ref = refs[2 * parts :]
    step = pl.program_id(0)
    part = step // (pl.num_programs(0) // parts)
    rows, width = out_ref.shape
    lines = rows // width
    diagonal = diagonal_of(width)
    for j in range(lines):
        at = slice(j * width, (j + 1) * width)
        grads = refs[0][at, :].astype(jnp.float32) + refs[1][at, :].astype(jnp.float32)
        for i in range(1, parts):
            later = refs[2 * i][at, :].astype(jnp.float32) + refs[2 * i + 1][at, :].astype(jnp.float32)
            grads = jnp.where(part >= i, later, grads)
        fresh_accum = fresh_accum_of(grads, accum_ref[pl.ds(step * lines + j, 1), :], diagonal)
        out_ref[at, :] = table_ref[at, :] - LEARN * grads / jnp.sqrt(fresh_accum + EPSILON)


def finished_table(halves, accum, table):
    row_count, width = table.shape
    parts = len(halves)
    tile = min(512, row_count // parts)
    per_part = row_count // parts // tile
    specs = [
        pl.BlockSpec((tile, width), functools.partial(lambda i, k: (jnp.clip(k - i * per_part, 0, per_part - 1), 0), i))
        for i in range(parts)
    ]
    rows_spec = pl.BlockSpec((tile, width), lambda k: (k, 0))
    return pl.pallas_call(
        functools.partial(finish_kernel, parts=parts),
        grid=(row_count // tile,),
        in_specs=[spec for spec in specs for _ in range(2)]
        + [pl.BlockSpec(accum.shape, lambda k: (0, 0)), rows_spec],
        out_specs=rows_spec,
        out_shape=jax.ShapeDtypeStruct(table.shape, jnp.float32),
    )(*[term for pair in halves for term in pair], accum, table)


def parity_kernel(slot_ref, peer_slot_ref, delta_ref, peer_delta_ref, *refs, base, holder_rows, dp_count, tile, last):
    refs, total_ref = refs[:-1], refs[-1]
    if base > 0:
        start_ref, refs, held_ref, sem = refs[0], refs[1:-2], refs[-2], refs[-1]
        copy = pltpu.make_async_copy(start_ref, held_ref, sem)
        copy.start()
    core, chip, dp_index = position()
    part_count = holder_rows // dp_count
    line_width = slot_ref.shape[1]
    width = delta_ref.shape[1]
    for k in range(delta_ref.shape[0] // tile):
        first = (base + k * tile) // line_width
        slot = jnp.concatenate(
            [
                ref[first + i : first + i + 1, :]
                for ref in (slot_ref, peer_slot_ref)
                for i in range(tile // line_width)
            ],
            axis=1,
        )
        holder, offset = split_index(slot, holder_rows)
        part, offset = split_index(offset, part_count)
        mine = (lax.bitwise_and(holder, 1) == core) & (part == dp_index)
        target = lax.bitwise_xor(lax.shift_right_arithmetic(holder, 1), chip) * part_count + offset
        at = slice(k * tile, (k + 1) * tile)
        rows = jnp.concatenate([delta_ref[at, :], peer_delta_ref[at, :]], axis=0)
        add_segments(total_ref, jnp.where(mine, target, -1), rows, k == 0)
    if base > 0:
        copy.wait()
        total_ref[...] += held_ref[...]
    if not last:
        refs[-1][...] = total_ref[...]
        return
    low_count = total_ref.shape[0]
    out_refs = refs[-(low_count * SPLIT // part_count) :]
    for i, out_ref in enumerate(out_refs):
        block, low = divmod(i * part_count, low_count)
        out_ref[...] = total_ref[
            low : low + part_count, block * width : (block + 1) * width
        ].astype(out_ref.dtype)


def parity_changes(slot, peer_slot, delta, peer_delta, base, holder_rows, dp_count, chip_count, start, last):
    width = delta.shape[1]
    part_count = holder_rows // dp_count
    segment_count = chip_count * part_count
    held = pltpu.VMEM((segment_count // SPLIT, SPLIT * width), jnp.float32)
    return pl.pallas_call(
        functools.partial(
            parity_kernel, base=base, holder_rows=holder_rows, dp_count=dp_count,
            tile=min(1024, delta.shape[0]), last=last,
        ),
        in_specs=[VMEM] * 4 + [pl.BlockSpec(memory_space=pl.ANY)] * len(start),
        out_specs=[VMEM] * chip_count if last else VMEM,
        out_shape=[pltpu.VMEM((part_count, width), jnp.bfloat16)] * chip_count
        if last
        else jax.ShapeDtypeStruct(held.shape, held.dtype),
        scratch_shapes=([held, pltpu.SemaphoreType.DMA] if start else []) + [held],
    )(*map(near, (slot, peer_slot, delta, peer_delta)), *start)


def on_device(owners, local_rows, grad_pooled, table, accum, parity, parity_slot):
    table_count = lax.axis_size("table")
    dp_count = lax.axis_size("dp")
    chip_count = table_count // 2
    half = table_count // 2
    bag_count, _ = owners.shape
    row_count, width = table.shape
    parity_count = parity.shape[0]
    dp_index = lax.axis_index("dp")
    same_core = [list(range(c, table_count, 2)) for c in range(2)]

    def swap(values, distance):
        return lax.ppermute(values, "table", [(i, i ^ distance) for i in range(table_count)])

    def exchange(values):
        return lax.all_to_all(
            values, "table", split_axis=0, concat_axis=0, axis_index_groups=same_core, tiled=True
        )

    far_grads = swap(grad_pooled, half)

    devices = jnp.arange(table_count, dtype=jnp.int32)[:, None, None, None]
    named = owners.T[None, None] == devices
    requests = jnp.max(jnp.where(named, local_rows.T[None, None], -1), axis=2)
    asked = lax.all_to_all(requests, "table", split_axis=0, concat_axis=0, tiled=True)
    line_width = 4 * width
    slot_lines = parity_slot.reshape(-1, line_width)
    peer_slot_lines = swap(slot_lines, 1)

    grads = [jnp.concatenate([grad_pooled, far_grads], axis=0)]
    for k in range(1, chip_count // 2):
        grads.append(swap(grads[0], 2 * k))
    peer_grads = []
    for values in grads:
        peer_grads.append(swap(values, 1))

    own_named, peer_named = named_rows(asked, table)
    found = swap(peer_named, 1)
    fetched = (own_named.astype(jnp.float32) + found.astype(jnp.float32)).astype(jnp.bfloat16)

    halves, bases = [], []
    for part, share in enumerate(PARTS):
        part_rows = row_count // share
        bases.append(sum(row_count // other for other in PARTS[:part]))
        mine = row_gradients(asked, grads, peer_grads, bases[part], part_rows)
        distance = 1
        other = lax.ppermute(mine, "dp", [(i, i ^ 1) for i in range(dp_count)])
        while 2 * distance < dp_count:
            distance *= 2
            mine = (mine.astype(jnp.float32) + other.astype(jnp.float32)).astype(jnp.bfloat16)
            other = lax.ppermute(mine, "dp", [(i, i ^ distance) for i in range(dp_count)])
        halves.append((mine, other))

    returned = exchange(fetched.reshape(chip_count, bag_count, width))

    accums, changes = [], []
    accum_lines = accum.reshape(-1, width)
    for part, (mine, other) in enumerate(halves):
        fresh_accum, delta = changes_of(mine, other, accum_lines, bases[part])
        accums.append(fresh_accum)
        peer_delta = swap(delta, 1)
        changes = parity_changes(
            slot_lines, peer_slot_lines, delta, peer_delta, bases[part],
            parity_count, dp_count, chip_count, changes, part == len(PARTS) - 1,
        )
        if part < len(PARTS) - 1:
            changes = [changes]
    arrived = [changes[0]]
    for k in range(1, chip_count):
        arrived.append(swap(changes[k], 2 * k))
    pooled = jnp.sum(returned.astype(jnp.float32), axis=0).astype(jnp.bfloat16)
    new_table = finished_table(halves, accum_lines, table)
    new_accum = jnp.concatenate(accums, axis=0).reshape(row_count)
    part = sum(values.astype(jnp.float32) for values in arrived).astype(jnp.bfloat16)
    if dp_count == 2:
        other = lax.ppermute(part, "dp", [(0, 1), (1, 0)])
        parts = jnp.where(dp_index == 0, jnp.stack([part, other]), jnp.stack([other, part]))
    else:
        parts = lax.all_gather(part, "dp", axis=0)
    new_parity = parity + parts.reshape(parity_count, width).astype(jnp.float32)
    return (pooled, new_table, new_accum, new_parity)


def solution(mesh):
    in_specs = (
        P(("table", "dp"), None),
        P(("table", "dp"), None),
        P(("table", "dp"), None),
        P("table", None),
        P("table"),
        P("table", None),
        P("table"),
    )
    out_specs = (P(("table", "dp"), None), P("table", None), P("table"), P("table", None))

    return jax.shard_map(on_device, mesh=mesh, in_specs=in_specs, out_specs=out_specs, check_vma=False)
```

```python
import functools
import jax
import jax.numpy as jnp
from jax import lax
from jax.experimental import pallas as pl
from jax.experimental.pallas import tpu as pltpu
from jax.sharding import PartitionSpec as P

LEARN = 0.5
EPSILON = 1e-06
SPLIT = 4
PARTS = (2, 2)
SUM_PART = 1
NEAR_BYTES = 1 << 21
VMEM = pl.BlockSpec(memory_space=pltpu.VMEM)


def near(values, copies=1):
    if copies * values.size * values.dtype.itemsize > NEAR_BYTES:
        return values
    return pltpu.with_memory_space_constraint(values, pltpu.MemorySpace.VMEM)


def column_of(row, lanes):
    return jnp.broadcast_to(row, (lanes, row.shape[1])).T


def bits_of(count):
    assert count & (count - 1) == 0
    return count.bit_length() - 1


def split_index(index, low_count):
    return lax.shift_right_arithmetic(index, bits_of(low_count)), lax.bitwise_and(index, low_count - 1)


def position():
    device = lax.axis_index("table")
    return lax.bitwise_and(device, 1), lax.shift_right_logical(device, 1), lax.axis_index("dp")


def add_segments(total_ref, index, rows, first):
    low_count, spread_width = total_ref.shape
    width = rows.shape[1]
    split = spread_width // width
    block, low = split_index(index, low_count)
    low = jnp.where((block < 0) | (block >= split), -1, low)
    hits = (
        (lax.broadcasted_iota(jnp.int32, (low_count, index.shape[1]), 0) == low)
        .astype(jnp.float32)
        .astype(jnp.bfloat16)
    )
    block_column = column_of(block, width)
    rows = rows.astype(jnp.float32)
    spread = jnp.concatenate(
        [jnp.where(block_column == i, rows, 0.0).astype(jnp.bfloat16) for i in range(split)], axis=1
    )
    part = jnp.dot(hits, spread, preferred_element_type=jnp.float32)
    if first:
        total_ref[...] = part
    else:
        total_ref[...] += part


def put_segments(out_ref, total_ref):
    low_count, width = total_ref.shape[0], out_ref.shape[1]
    for i in range(total_ref.shape[1] // width):
        out_ref[i * low_count : (i + 1) * low_count, :] = total_ref[
            :, i * width : (i + 1) * width
        ].astype(out_ref.dtype)


def segment_kernel(asked_ref, *refs, base, count):
    grad_refs, refs = refs[: 2 * count], refs[2 * count :]
    if len(refs) > 2:
        first_ref, second_ref, out_ref, sum_ref, total_ref, terms_ref, sums_ref, in_sems, out_sems = refs
        chunk = sums_ref.shape[0] // count
        at = [pl.ds(k * chunk, chunk) for k in range(count)]
        loads = [
            [
                pltpu.make_async_copy(ref.at[at[k], :], terms_ref.at[i, at[k], :], in_sems.at[i, k])
                for i, ref in enumerate((first_ref, second_ref))
            ]
            for k in range(count)
        ]
        stores = [
            pltpu.make_async_copy(sums_ref.at[at[k], :], sum_ref.at[at[k], :], out_sems.at[k])
            for k in range(count)
        ]
        for pair in loads:
            for copy in pair:
                copy.start()
    else:
        (out_ref, total_ref), stores = refs, []
    core, chip, _ = position()
    for k in range(count):
        sources = [2 * (chip ^ k ^ far) + (core ^ side) for side in range(2) for far in (0, count)]
        index = jnp.concatenate([asked_ref[source] for source in sources], axis=1) - base
        rows = jnp.concatenate([grad_refs[k][...], grad_refs[count + k][...]], axis=0)
        add_segments(total_ref, index, rows, k == 0)
        if stores:
            for copy in loads[k]:
                copy.wait()
            here = slice(k * chunk, (k + 1) * chunk)
            terms = [terms_ref[i, here, :].astype(jnp.float32) for i in range(2)]
            sums_ref[here, :] = (terms[0] + terms[1]).astype(jnp.bfloat16)
            stores[k].start()
    put_segments(out_ref, total_ref)
    for copy in stores:
        copy.wait()


def row_gradients(asked, grads, peer_grads, base, row_count, terms=()):
    width = grads[0].shape[1]
    count = len(grads)
    split = SPLIT if row_count > 4 * 256 else SPLIT // 2
    anywhere = pl.BlockSpec(memory_space=pl.ANY)
    out_shape = [pltpu.VMEM((row_count, width), jnp.bfloat16)]
    scratch_shapes = [pltpu.VMEM((row_count // split, split * width), jnp.float32)]
    if terms:
        shape = terms[0].shape
        out_shape.append(jax.ShapeDtypeStruct(shape, jnp.bfloat16))
        scratch_shapes += [
            pltpu.VMEM((2,) + shape, jnp.bfloat16),
            pltpu.VMEM(shape, jnp.bfloat16),
            pltpu.SemaphoreType.DMA((2, count)),
            pltpu.SemaphoreType.DMA((count,)),
        ]
    return pl.pallas_call(
        functools.partial(segment_kernel, base=base, count=count),
        in_specs=[VMEM] * (1 + 2 * count) + [anywhere] * len(terms),
        out_specs=[VMEM] + [anywhere] * (1 if terms else 0),
        out_shape=out_shape,
        scratch_shapes=scratch_shapes,
    )(near(asked), *[near(g, 2 * count) for g in (*grads, *peer_grads)], *terms)


def gather_kernel(asked_ref, table_ref, *refs, together):
    out_refs, (arrived_ref, held_ref, sems) = refs[:2], refs[2:]
    low_count, width = held_ref.shape[0], table_ref.shape[1]
    bags = asked_ref.shape[2]
    core, _, _ = position()
    copies = []
    for i in range(SPLIT):
        at = pl.ds(i * low_count, low_count)
        copies.append(pltpu.make_async_copy(table_ref.at[at, :], arrived_ref.at[at, :], sems.at[i]))
        copies[i].start()
    for i in range(SPLIT):
        copies[i].wait()
        rows = arrived_ref[i * low_count : (i + 1) * low_count, :]
        held_ref[:, i * width : (i + 1) * width] = rows.astype(jnp.bfloat16)
    lane = lax.broadcasted_iota(jnp.int32, (together * bags, width), 1)
    for side in (1, 0):
        for j in range(0, asked_ref.shape[0] // 2, together):
            index = jnp.concatenate(
                [asked_ref[2 * (j + i) + (core ^ side)] for i in range(together)], axis=1
            )
            block, low = split_index(column_of(index, width), low_count)
            hits = jnp.concatenate(
                [
                    (lane == low - first).astype(jnp.float32).astype(jnp.bfloat16)
                    for first in range(0, low_count, width)
                ],
                axis=1,
            )
            found = jnp.dot(hits, held_ref[...], preferred_element_type=jnp.float32)
            row = jnp.where(block == 0, found[:, :width], 0.0)
            for i in range(1, SPLIT):
                row = jnp.where(block == i, found[:, i * width : (i + 1) * width], row)
            out_refs[side][j * bags : (j + together) * bags, :] = row.astype(jnp.bfloat16)


def named_rows(asked, table):
    row_count, width = table.shape
    sources, _, bags = asked.shape
    rows = jax.ShapeDtypeStruct((sources // 2 * bags, width), jnp.bfloat16)
    return pl.pallas_call(
        functools.partial(gather_kernel, together=2),
        in_specs=[VMEM, pl.BlockSpec(memory_space=pl.ANY)],
        out_specs=[VMEM, VMEM],
        out_shape=[rows, rows],
        scratch_shapes=[
            pltpu.VMEM(table.shape, table.dtype),
            pltpu.VMEM((row_count // SPLIT, SPLIT * width), jnp.bfloat16),
            pltpu.SemaphoreType.DMA((SPLIT,)),
        ],
    )(near(asked), table)


def diagonal_of(width):
    rows = lax.broadcasted_iota(jnp.int32, (width, width), 0)
    return rows == lax.broadcasted_iota(jnp.int32, (width, width), 1)


def fresh_accum_of(grads, accum_line, diagonal):
    width = grads.shape[1]
    rest, terms = grads * grads + jnp.where(diagonal, accum_line * width, 0.0), []
    for _ in range(3):
        terms.append(rest.astype(jnp.bfloat16))
        rest = rest - terms[-1].astype(jnp.float32)
    ones = jnp.ones((3 * width, width), jnp.bfloat16)
    sums = jnp.dot(jnp.concatenate(terms, axis=1), ones, preferred_element_type=jnp.float32)
    return sums * (1.0 / width)


def change_kernel(own_ref, other_ref, accum_ref, new_accum_ref, delta_ref, *, base):
    rows, width = own_ref.shape
    diagonal = diagonal_of(width)
    for j in range(rows // width):
        at = slice(j * width, (j + 1) * width)
        line = base // width + j
        grads = own_ref[at, :].astype(jnp.float32) + other_ref[at, :].astype(jnp.float32)
        fresh_accum = fresh_accum_of(grads, accum_ref[line : line + 1, :], diagonal)
        delta_ref[at, :] = (-LEARN * grads / jnp.sqrt(fresh_accum + EPSILON)).astype(jnp.bfloat16)
        new_accum_ref[j : j + 1, :] = jnp.sum(
            jnp.where(diagonal, fresh_accum, 0.0), axis=0, keepdims=True
        )


def changes_of(own, other, accum, base):
    rows, width = own.shape
    return pl.pallas_call(
        functools.partial(change_kernel, base=base),
        in_specs=[VMEM] * 3,
        out_specs=[VMEM, VMEM],
        out_shape=[
            jax.ShapeDtypeStruct((rows // width, width), jnp.float32),
            pltpu.VMEM((rows, width), jnp.bfloat16),
        ],
    )(*map(near, (own, other, accum)))


def parity_kernel(*refs, base, holder_rows, dp_count, tile, last):
    slot_ref, peer_slot_ref, delta_ref, peer_delta_ref, table_ref = refs[:5]
    scratch, refs = refs[-5:], refs[5:-5]
    total_ref, old_ref, fresh_ref, load_sems, store_sems = scratch
    steps = delta_ref.shape[0] // tile
    if base > 0:
        start_ref, refs, held_ref, sem = refs[0], refs[2:-2], refs[-2], refs[-1]
        copy = pltpu.make_async_copy(start_ref, held_ref, sem)
        copy.start()
    new_table_ref, out_refs = refs[0], refs[1:]
    loads, stores = [], []
    for k in range(steps):
        here, there = pl.ds(k * tile, tile), pl.ds(base + k * tile, tile)
        loads.append(pltpu.make_async_copy(table_ref.at[there, :], old_ref.at[here, :], load_sems.at[k]))
        stores.append(
            pltpu.make_async_copy(fresh_ref.at[here, :], new_table_ref.at[there, :], store_sems.at[k])
        )
        loads[k].start()
    core, chip, dp_index = position()
    part_count = holder_rows // dp_count
    line_width = slot_ref.shape[1]
    width = delta_ref.shape[1]
    for k in range(steps):
        first = (base + k * tile) // line_width
        slot = jnp.concatenate(
            [
                ref[first + i : first + i + 1, :]
                for ref in (slot_ref, peer_slot_ref)
                for i in range(tile // line_width)
            ],
            axis=1,
        )
        holder, offset = split_index(slot, holder_rows)
        part, offset = split_index(offset, part_count)
        mine = (lax.bitwise_and(holder, 1) == core) & (part == dp_index)
        target = lax.bitwise_xor(lax.shift_right_arithmetic(holder, 1), chip) * part_count + offset
        at = slice(k * tile, (k + 1) * tile)
        rows = jnp.concatenate([delta_ref[at, :], peer_delta_ref[at, :]], axis=0)
        add_segments(total_ref, jnp.where(mine, target, -1), rows, k == 0)
        loads[k].wait()
        fresh_ref[at, :] = old_ref[at, :] + delta_ref[at, :].astype(jnp.float32)
        stores[k].start()
    if base > 0:
        copy.wait()
        total_ref[...] += held_ref[...]
    if last:
        low_count = total_ref.shape[0]
        for i, out_ref in enumerate(out_refs):
            block, low = divmod(i * part_count, low_count)
            out_ref[...] = total_ref[
                low : low + part_count, block * width : (block + 1) * width
            ].astype(out_ref.dtype)
    else:
        out_refs[0][...] = total_ref[...]
    for store in stores:
        store.wait()


def parity_changes(slot, peer_slot, delta, peer_delta, table, base, holder_rows, dp_count, chip_count, start, new_table, last):
    rows, width = delta.shape
    part_count = holder_rows // dp_count
    segment_count = chip_count * part_count
    held = pltpu.VMEM((segment_count // SPLIT, SPLIT * width), jnp.float32)
    anywhere = pl.BlockSpec(memory_space=pl.ANY)
    tile = min(1024, rows)
    changes = [pltpu.VMEM((part_count, width), jnp.bfloat16)] * chip_count
    if not last:
        changes = [jax.ShapeDtypeStruct(held.shape, held.dtype)]
    return pl.pallas_call(
        functools.partial(
            parity_kernel, base=base, holder_rows=holder_rows, dp_count=dp_count, tile=tile, last=last
        ),
        in_specs=[VMEM] * 4 + [anywhere] * (1 + len(start) + len(new_table)),
        out_specs=[anywhere] + [VMEM] * len(changes),
        out_shape=[jax.ShapeDtypeStruct(table.shape, jnp.float32)] + changes,
        scratch_shapes=([held, pltpu.SemaphoreType.DMA] if start else [])
        + [
            held,
            pltpu.VMEM((rows, width), jnp.float32),
            pltpu.VMEM((rows, width), jnp.float32),
            pltpu.SemaphoreType.DMA((rows // tile,)),
            pltpu.SemaphoreType.DMA((rows // tile,)),
        ],
        input_output_aliases={6: 0} if new_table else {},
    )(*map(near, (slot, peer_slot, delta, peer_delta)), table, *start, *new_table)


def on_device(owners, local_rows, grad_pooled, table, accum, parity, parity_slot):
    table_count = lax.axis_size("table")
    dp_count = lax.axis_size("dp")
    chip_count = table_count // 2
    half = table_count // 2
    bag_count, _ = owners.shape
    row_count, width = table.shape
    parity_count = parity.shape[0]
    dp_index = lax.axis_index("dp")
    same_core = [list(range(c, table_count, 2)) for c in range(2)]

    def swap(values, distance):
        return lax.ppermute(values, "table", [(i, i ^ distance) for i in range(table_count)])

    def exchange(values):
        return lax.all_to_all(
            values, "table", split_axis=0, concat_axis=0, axis_index_groups=same_core, tiled=True
        )

    far_grads = swap(grad_pooled, half)

    devices = jnp.arange(table_count, dtype=jnp.int32)[:, None, None, None]
    named = owners.T[None, None] == devices
    requests = jnp.max(jnp.where(named, local_rows.T[None, None], -1), axis=2)
    asked = lax.all_to_all(requests, "table", split_axis=0, concat_axis=0, tiled=True)
    line_width = 4 * width
    slot_lines = parity_slot.reshape(-1, line_width)
    peer_slot_lines = swap(slot_lines, 1)

    grads = [jnp.concatenate([grad_pooled, far_grads], axis=0)]
    for k in range(1, chip_count // 2):
        grads.append(swap(grads[0], 2 * k))
    peer_grads = []
    for values in grads:
        peer_grads.append(swap(values, 1))

    own_named, peer_named = named_rows(asked, table)
    found = swap(peer_named, 1)

    halves, bases = [], []
    for part, share in enumerate(PARTS):
        part_rows = row_count // share
        bases.append(sum(row_count // other for other in PARTS[:part]))
        terms = (own_named, found) if part == SUM_PART else ()
        mine, *sums = row_gradients(asked, grads, peer_grads, bases[part], part_rows, terms)
        if sums:
            fetched = sums[0]
        distance = 1
        other = lax.ppermute(mine, "dp", [(i, i ^ 1) for i in range(dp_count)])
        while 2 * distance < dp_count:
            distance *= 2
            mine = (mine.astype(jnp.float32) + other.astype(jnp.float32)).astype(jnp.bfloat16)
            other = lax.ppermute(mine, "dp", [(i, i ^ distance) for i in range(dp_count)])
        halves.append((mine, other))

    returned = exchange(fetched.reshape(chip_count, bag_count, width))

    accums, changes, new_table = [], [], []
    accum_lines = accum.reshape(-1, width)
    for part, (mine, other) in enumerate(halves):
        fresh_accum, delta = changes_of(mine, other, accum_lines, bases[part])
        accums.append(fresh_accum)
        peer_delta = swap(delta, 1)
        new_table, *changes = parity_changes(
            slot_lines, peer_slot_lines, delta, peer_delta, table, bases[part],
            parity_count, dp_count, chip_count, changes, new_table, part == len(PARTS) - 1,
        )
        new_table = [new_table]
    arrived = [changes[0]]
    for k in range(1, chip_count):
        arrived.append(swap(changes[k], 2 * k))
    pooled = jnp.sum(returned.astype(jnp.float32), axis=0).astype(jnp.bfloat16)
    new_accum = jnp.concatenate(accums, axis=0).reshape(row_count)
    part = sum(values.astype(jnp.float32) for values in arrived).astype(jnp.bfloat16)
    if dp_count == 2:
        other = lax.ppermute(part, "dp", [(0, 1), (1, 0)])
        parts = jnp.where(dp_index == 0, jnp.stack([part, other]), jnp.stack([other, part]))
    else:
        parts = lax.all_gather(part, "dp", axis=0)
    new_parity = parity + parts.reshape(parity_count, width).astype(jnp.float32)
    return (pooled, new_table[0], new_accum, new_parity)


def solution(mesh):
    in_specs = (
        P(("table", "dp"), None),
        P(("table", "dp"), None),
        P(("table", "dp"), None),
        P("table", None),
        P("table"),
        P("table", None),
        P("table"),
    )
    out_specs = (P(("table", "dp"), None), P("table", None), P("table"), P("table", None))

    return jax.shard_map(on_device, mesh=mesh, in_specs=in_specs, out_specs=out_specs, check_vma=False)
```

```python
import functools
import jax
import jax.numpy as jnp
from jax import lax
from jax.experimental import pallas as pl
from jax.experimental.pallas import tpu as pltpu
from jax.sharding import PartitionSpec as P

LEARN = 0.5
EPSILON = 1e-06
SPLIT = 4
PARTS = (2, 2)
GRANT = pltpu.CompilerParams(vmem_limit_bytes=56 << 20)
SUM_PART = 1
NEAR_BYTES = 1 << 21
VMEM = pl.BlockSpec(memory_space=pltpu.VMEM)


def near(values, copies=1):
    if copies * values.size * values.dtype.itemsize > NEAR_BYTES:
        return values
    return pltpu.with_memory_space_constraint(values, pltpu.MemorySpace.VMEM)


def column_of(row, lanes):
    return jnp.broadcast_to(row, (lanes, row.shape[1])).T


def bits_of(count):
    assert count & (count - 1) == 0
    return count.bit_length() - 1


def split_index(index, low_count):
    return lax.shift_right_arithmetic(index, bits_of(low_count)), lax.bitwise_and(index, low_count - 1)


def position():
    device = lax.axis_index("table")
    return lax.bitwise_and(device, 1), lax.shift_right_logical(device, 1), lax.axis_index("dp")


def add_segments(total_ref, index, rows, first):
    low_count, spread_width = total_ref.shape
    width = rows.shape[1]
    split = spread_width // width
    block, low = split_index(index, low_count)
    low = jnp.where((block < 0) | (block >= split), -1, low)
    hits = (
        (lax.broadcasted_iota(jnp.int32, (low_count, index.shape[1]), 0) == low)
        .astype(jnp.float32)
        .astype(jnp.bfloat16)
    )
    block_column = column_of(block, width)
    rows = rows.astype(jnp.float32)
    spread = jnp.concatenate(
        [jnp.where(block_column == i, rows, 0.0).astype(jnp.bfloat16) for i in range(split)], axis=1
    )
    part = jnp.dot(hits, spread, preferred_element_type=jnp.float32)
    if first:
        total_ref[...] = part
    else:
        total_ref[...] += part


def put_segments(out_ref, total_ref):
    low_count, width = total_ref.shape[0], out_ref.shape[1]
    for i in range(total_ref.shape[1] // width):
        out_ref[i * low_count : (i + 1) * low_count, :] = total_ref[
            :, i * width : (i + 1) * width
        ].astype(out_ref.dtype)


def segment_kernel(asked_ref, *refs, base, count):
    grad_refs, refs = refs[: 2 * count], refs[2 * count :]
    if len(refs) > 2:
        first_ref, second_ref, out_ref, sum_ref, total_ref, terms_ref, sums_ref, in_sems, out_sems = refs
        chunk = sums_ref.shape[0] // count
        at = [pl.ds(k * chunk, chunk) for k in range(count)]
        loads = [
            [
                pltpu.make_async_copy(ref.at[at[k], :], terms_ref.at[i, at[k], :], in_sems.at[i, k])
                for i, ref in enumerate((first_ref, second_ref))
            ]
            for k in range(count)
        ]
        stores = [
            pltpu.make_async_copy(sums_ref.at[at[k], :], sum_ref.at[at[k], :], out_sems.at[k])
            for k in range(count)
        ]
        for pair in loads:
            for copy in pair:
                copy.start()
    else:
        (out_ref, total_ref), stores = refs, []
    core, chip, _ = position()
    for k in range(count):
        sources = [2 * (chip ^ k ^ far) + (core ^ side) for side in range(2) for far in (0, count)]
        index = jnp.concatenate([asked_ref[source] for source in sources], axis=1) - base
        rows = jnp.concatenate([grad_refs[k][...], grad_refs[count + k][...]], axis=0)
        add_segments(total_ref, index, rows, k == 0)
        if stores:
            for copy in loads[k]:
                copy.wait()
            here = slice(k * chunk, (k + 1) * chunk)
            terms = [terms_ref[i, here, :].astype(jnp.float32) for i in range(2)]
            sums_ref[here, :] = (terms[0] + terms[1]).astype(jnp.bfloat16)
            stores[k].start()
    put_segments(out_ref, total_ref)
    for copy in stores:
        copy.wait()


def row_gradients(asked, grads, peer_grads, base, row_count, terms=()):
    width = grads[0].shape[1]
    count = len(grads)
    split = SPLIT if row_count > 4 * 256 else SPLIT // 2
    anywhere = pl.BlockSpec(memory_space=pltpu.HBM)
    out_shape = [pltpu.VMEM((row_count, width), jnp.bfloat16)]
    scratch_shapes = [pltpu.VMEM((row_count // split, split * width), jnp.float32)]
    if terms:
        shape = terms[0].shape
        out_shape.append(jax.ShapeDtypeStruct(shape, jnp.bfloat16))
        scratch_shapes += [
            pltpu.VMEM((2,) + shape, jnp.bfloat16),
            pltpu.VMEM(shape, jnp.bfloat16),
            pltpu.SemaphoreType.DMA((2, count)),
            pltpu.SemaphoreType.DMA((count,)),
        ]
    return pl.pallas_call(
        functools.partial(segment_kernel, base=base, count=count),
        compiler_params=GRANT,
        in_specs=[VMEM] * (1 + 2 * count) + [anywhere] * len(terms),
        out_specs=[VMEM] + [anywhere] * (1 if terms else 0),
        out_shape=out_shape,
        scratch_shapes=scratch_shapes,
    )(near(asked), *[near(g, 2 * count) for g in (*grads, *peer_grads)], *terms)


def gather_kernel(asked_ref, table_ref, *refs, together):
    out_refs, (arrived_ref, held_ref, sems) = refs[:2], refs[2:]
    low_count, width = held_ref.shape[0], table_ref.shape[1]
    bags = asked_ref.shape[2]
    core, _, _ = position()
    copies = []
    for i in range(SPLIT):
        at = pl.ds(i * low_count, low_count)
        copies.append(pltpu.make_async_copy(table_ref.at[at, :], arrived_ref.at[at, :], sems.at[i]))
        copies[i].start()
    for i in range(SPLIT):
        copies[i].wait()
        rows = arrived_ref[i * low_count : (i + 1) * low_count, :]
        held_ref[:, i * width : (i + 1) * width] = rows.astype(jnp.bfloat16)
    lane = lax.broadcasted_iota(jnp.int32, (together * bags, width), 1)
    for side in (1, 0):
        for j in range(0, asked_ref.shape[0] // 2, together):
            index = jnp.concatenate(
                [asked_ref[2 * (j + i) + (core ^ side)] for i in range(together)], axis=1
            )
            block, low = split_index(column_of(index, width), low_count)
            hits = jnp.concatenate(
                [
                    (lane == low - first).astype(jnp.float32).astype(jnp.bfloat16)
                    for first in range(0, low_count, width)
                ],
                axis=1,
            )
            found = jnp.dot(hits, held_ref[...], preferred_element_type=jnp.float32)
            row = jnp.where(block == 0, found[:, :width], 0.0)
            for i in range(1, SPLIT):
                row = jnp.where(block == i, found[:, i * width : (i + 1) * width], row)
            out_refs[side][j * bags : (j + together) * bags, :] = row.astype(jnp.bfloat16)


def named_rows(asked, table):
    row_count, width = table.shape
    sources, _, bags = asked.shape
    rows = jax.ShapeDtypeStruct((sources // 2 * bags, width), jnp.bfloat16)
    return pl.pallas_call(
        functools.partial(gather_kernel, together=2),
        compiler_params=GRANT,
        in_specs=[VMEM, pl.BlockSpec(memory_space=pltpu.HBM)],
        out_specs=[VMEM, VMEM],
        out_shape=[rows, rows],
        scratch_shapes=[
            pltpu.VMEM(table.shape, table.dtype),
            pltpu.VMEM((row_count // SPLIT, SPLIT * width), jnp.bfloat16),
            pltpu.SemaphoreType.DMA((SPLIT,)),
        ],
    )(near(asked), table)


def diagonal_of(width):
    rows = lax.broadcasted_iota(jnp.int32, (width, width), 0)
    return rows == lax.broadcasted_iota(jnp.int32, (width, width), 1)


def fresh_accum_of(grads, accum_line, diagonal):
    width = grads.shape[1]
    rest, terms = grads * grads + jnp.where(diagonal, accum_line * width, 0.0), []
    for _ in range(3):
        terms.append(rest.astype(jnp.bfloat16))
        rest = rest - terms[-1].astype(jnp.float32)
    ones = jnp.ones((3 * width, width), jnp.bfloat16)
    sums = jnp.dot(jnp.concatenate(terms, axis=1), ones, preferred_element_type=jnp.float32)
    return sums * (1.0 / width)


def change_kernel(own_ref, other_ref, accum_ref, new_accum_ref, delta_ref, *, base):
    rows, width = own_ref.shape
    diagonal = diagonal_of(width)
    for j in range(rows // width):
        at = slice(j * width, (j + 1) * width)
        line = base // width + j
        grads = own_ref[at, :].astype(jnp.float32) + other_ref[at, :].astype(jnp.float32)
        fresh_accum = fresh_accum_of(grads, accum_ref[line : line + 1, :], diagonal)
        delta_ref[at, :] = (-LEARN * grads / jnp.sqrt(fresh_accum + EPSILON)).astype(jnp.bfloat16)
        new_accum_ref[j : j + 1, :] = jnp.sum(
            jnp.where(diagonal, fresh_accum, 0.0), axis=0, keepdims=True
        )


def changes_of(own, other, accum, base):
    rows, width = own.shape
    return pl.pallas_call(
        functools.partial(change_kernel, base=base),
        compiler_params=GRANT,
        in_specs=[VMEM] * 3,
        out_specs=[VMEM, VMEM],
        out_shape=[
            jax.ShapeDtypeStruct((rows // width, width), jnp.float32),
            pltpu.VMEM((rows, width), jnp.bfloat16),
        ],
    )(*map(near, (own, other, accum)))


def parity_kernel(*refs, base, holder_rows, dp_count, tile, last):
    slot_ref, peer_slot_ref, delta_ref, peer_delta_ref, table_ref = refs[:5]
    scratch, refs = refs[-5:], refs[5:-5]
    total_ref, old_ref, fresh_ref, load_sems, store_sems = scratch
    steps = delta_ref.shape[0] // tile
    if base > 0:
        start_ref, refs, held_ref, sem = refs[0], refs[2:-2], refs[-2], refs[-1]
        copy = pltpu.make_async_copy(start_ref, held_ref, sem)
        copy.start()
    new_table_ref, out_refs = refs[0], refs[1:]
    loads, stores = [], []
    for k in range(steps):
        here, there = pl.ds(k * tile, tile), pl.ds(base + k * tile, tile)
        loads.append(pltpu.make_async_copy(table_ref.at[there, :], old_ref.at[here, :], load_sems.at[k]))
        stores.append(
            pltpu.make_async_copy(fresh_ref.at[here, :], new_table_ref.at[there, :], store_sems.at[k])
        )
        loads[k].start()
    core, chip, dp_index = position()
    part_count = holder_rows // dp_count
    line_width = slot_ref.shape[1]
    width = delta_ref.shape[1]
    for k in range(steps):
        first = (base + k * tile) // line_width
        slot = jnp.concatenate(
            [
                ref[first + i : first + i + 1, :]
                for ref in (slot_ref, peer_slot_ref)
                for i in range(tile // line_width)
            ],
            axis=1,
        )
        holder, offset = split_index(slot, holder_rows)
        part, offset = split_index(offset, part_count)
        mine = (lax.bitwise_and(holder, 1) == core) & (part == dp_index)
        target = lax.bitwise_xor(lax.shift_right_arithmetic(holder, 1), chip) * part_count + offset
        at = slice(k * tile, (k + 1) * tile)
        rows = jnp.concatenate([delta_ref[at, :], peer_delta_ref[at, :]], axis=0)
        add_segments(total_ref, jnp.where(mine, target, -1), rows, k == 0)
        loads[k].wait()
        fresh_ref[at, :] = old_ref[at, :] + delta_ref[at, :].astype(jnp.float32)
        stores[k].start()
    if base > 0:
        copy.wait()
        total_ref[...] += held_ref[...]
    if last:
        low_count = total_ref.shape[0]
        for i, out_ref in enumerate(out_refs):
            block, low = divmod(i * part_count, low_count)
            out_ref[...] = total_ref[
                low : low + part_count, block * width : (block + 1) * width
            ].astype(out_ref.dtype)
    else:
        out_refs[0][...] = total_ref[...]
    for store in stores:
        store.wait()


def parity_changes(slot, peer_slot, delta, peer_delta, table, base, holder_rows, dp_count, chip_count, start, new_table, last):
    rows, width = delta.shape
    part_count = holder_rows // dp_count
    segment_count = chip_count * part_count
    held = pltpu.VMEM((segment_count // SPLIT, SPLIT * width), jnp.float32)
    anywhere = pl.BlockSpec(memory_space=pltpu.HBM)
    tile = min(1024, rows)
    changes = [pltpu.VMEM((part_count, width), jnp.bfloat16)] * chip_count
    if not last:
        changes = [jax.ShapeDtypeStruct(held.shape, held.dtype)]
    return pl.pallas_call(
        functools.partial(
            parity_kernel, base=base, holder_rows=holder_rows, dp_count=dp_count, tile=tile, last=last
        ),
        compiler_params=GRANT,
        in_specs=[VMEM] * 4 + [anywhere] * (1 + len(start) + len(new_table)),
        out_specs=[anywhere] + [VMEM] * len(changes),
        out_shape=[jax.ShapeDtypeStruct(table.shape, jnp.float32)] + changes,
        scratch_shapes=([held, pltpu.SemaphoreType.DMA] if start else [])
        + [
            held,
            pltpu.VMEM((rows, width), jnp.float32),
            pltpu.VMEM((rows, width), jnp.float32),
            pltpu.SemaphoreType.DMA((rows // tile,)),
            pltpu.SemaphoreType.DMA((rows // tile,)),
        ],
        input_output_aliases={6: 0} if new_table else {},
    )(*map(near, (slot, peer_slot, delta, peer_delta)), table, *start, *new_table)


def on_device(owners, local_rows, grad_pooled, table, accum, parity, parity_slot):
    table_count = lax.axis_size("table")
    dp_count = lax.axis_size("dp")
    chip_count = table_count // 2
    half = table_count // 2
    bag_count, _ = owners.shape
    row_count, width = table.shape
    parity_count = parity.shape[0]
    dp_index = lax.axis_index("dp")
    same_core = [list(range(c, table_count, 2)) for c in range(2)]

    def swap(values, distance):
        return lax.ppermute(values, "table", [(i, i ^ distance) for i in range(table_count)])

    def exchange(values):
        return lax.all_to_all(
            values, "table", split_axis=0, concat_axis=0, axis_index_groups=same_core, tiled=True
        )

    far_grads = swap(grad_pooled, half)

    devices = jnp.arange(table_count, dtype=jnp.int32)[:, None, None, None]
    named = owners.T[None, None] == devices
    requests = jnp.max(jnp.where(named, local_rows.T[None, None], -1), axis=2)
    asked = lax.all_to_all(requests, "table", split_axis=0, concat_axis=0, tiled=True)
    line_width = 4 * width
    slot_lines = parity_slot.reshape(-1, line_width)
    peer_slot_lines = swap(slot_lines, 1)

    grads = [jnp.concatenate([grad_pooled, far_grads], axis=0)]
    for k in range(1, chip_count // 2):
        grads.append(swap(grads[0], 2 * k))
    peer_grads = []
    for values in grads:
        peer_grads.append(swap(values, 1))

    own_named, peer_named = named_rows(asked, table)
    found = swap(peer_named, 1)

    halves, bases = [], []
    for part, share in enumerate(PARTS):
        part_rows = row_count // share
        bases.append(sum(row_count // other for other in PARTS[:part]))
        terms = (own_named, found) if part == SUM_PART else ()
        mine, *sums = row_gradients(asked, grads, peer_grads, bases[part], part_rows, terms)
        if sums:
            fetched = sums[0]
        distance = 1
        other = lax.ppermute(mine, "dp", [(i, i ^ 1) for i in range(dp_count)])
        while 2 * distance < dp_count:
            distance *= 2
            mine = (mine.astype(jnp.float32) + other.astype(jnp.float32)).astype(jnp.bfloat16)
            other = lax.ppermute(mine, "dp", [(i, i ^ distance) for i in range(dp_count)])
        halves.append((mine, other))

    returned = exchange(fetched.reshape(chip_count, bag_count, width))

    accums, changes, new_table = [], [], []
    accum_lines = accum.reshape(-1, width)
    for part, (mine, other) in enumerate(halves):
        fresh_accum, delta = changes_of(mine, other, accum_lines, bases[part])
        accums.append(fresh_accum)
        peer_delta = swap(delta, 1)
        new_table, *changes = parity_changes(
            slot_lines, peer_slot_lines, delta, peer_delta, table, bases[part],
            parity_count, dp_count, chip_count, changes, new_table, part == len(PARTS) - 1,
        )
        new_table = [new_table]
    arrived = [changes[0]]
    for k in range(1, chip_count):
        arrived.append(swap(changes[k], 2 * k))
    pooled = jnp.sum(returned.astype(jnp.float32), axis=0).astype(jnp.bfloat16)
    new_accum = jnp.concatenate(accums, axis=0).reshape(row_count)
    part = sum(values.astype(jnp.float32) for values in arrived).astype(jnp.bfloat16)
    if dp_count == 2:
        other = lax.ppermute(part, "dp", [(0, 1), (1, 0)])
        parts = jnp.where(dp_index == 0, jnp.stack([part, other]), jnp.stack([other, part]))
    else:
        parts = lax.all_gather(part, "dp", axis=0)
    new_parity = parity + parts.reshape(parity_count, width).astype(jnp.float32)
    return (pooled, new_table[0], new_accum, new_parity)


def solution(mesh):
    in_specs = (
        P(("table", "dp"), None),
        P(("table", "dp"), None),
        P(("table", "dp"), None),
        P("table", None),
        P("table"),
        P("table", None),
        P("table"),
    )
    out_specs = (P(("table", "dp"), None), P("table", None), P("table"), P("table", None))

    return jax.shard_map(on_device, mesh=mesh, in_specs=in_specs, out_specs=out_specs, check_vma=False)
```

```python
import functools
import jax
import jax.numpy as jnp
from jax import lax
from jax.experimental import pallas as pl
from jax.experimental.pallas import tpu as pltpu
from jax.sharding import PartitionSpec as P

LEARN = 0.5
EPSILON = 1e-06
SPLIT = 4
PARTS = (2, 2)
GRANT = pltpu.CompilerParams(vmem_limit_bytes=56 << 20)
NEAR_BYTES = 1 << 21
VMEM = pl.BlockSpec(memory_space=pltpu.VMEM)


def near(values, copies=1):
    if copies * values.size * values.dtype.itemsize > NEAR_BYTES:
        return values
    return pltpu.with_memory_space_constraint(values, pltpu.MemorySpace.VMEM)


def column_of(row, lanes):
    return jnp.broadcast_to(row, (lanes, row.shape[1])).T


def bits_of(count):
    assert count & (count - 1) == 0
    return count.bit_length() - 1


def split_index(index, low_count):
    return lax.shift_right_arithmetic(index, bits_of(low_count)), lax.bitwise_and(index, low_count - 1)


def position():
    device = lax.axis_index("table")
    return lax.bitwise_and(device, 1), lax.shift_right_logical(device, 1), lax.axis_index("dp")


def add_segments(total_ref, index, rows, first):
    low_count, spread_width = total_ref.shape
    width = rows.shape[1]
    split = spread_width // width
    block, low = split_index(index, low_count)
    low = jnp.where((block < 0) | (block >= split), -1, low)
    hits = (
        (lax.broadcasted_iota(jnp.int32, (low_count, index.shape[1]), 0) == low)
        .astype(jnp.float32)
        .astype(jnp.bfloat16)
    )
    block_column = column_of(block, width)
    rows = rows.astype(jnp.float32)
    spread = jnp.concatenate(
        [jnp.where(block_column == i, rows, 0.0).astype(jnp.bfloat16) for i in range(split)], axis=1
    )
    part = jnp.dot(hits, spread, preferred_element_type=jnp.float32)
    if first:
        total_ref[...] = part
    else:
        total_ref[...] += part


def put_segments(out_ref, total_ref):
    low_count, width = total_ref.shape[0], out_ref.shape[1]
    for i in range(total_ref.shape[1] // width):
        out_ref[i * low_count : (i + 1) * low_count, :] = total_ref[
            :, i * width : (i + 1) * width
        ].astype(out_ref.dtype)


def segment_kernel(asked_ref, *refs, base, count):
    grad_refs, refs = refs[: 2 * count], refs[2 * count :]
    if len(refs) > 2:
        first_ref, second_ref, out_ref, sum_ref, total_ref, terms_ref, sums_ref, in_sems, out_sems = refs
        chunk = sums_ref.shape[0] // count
        at = [pl.ds(k * chunk, chunk) for k in range(count)]
        loads = [
            [
                pltpu.make_async_copy(ref.at[at[k], :], terms_ref.at[i, at[k], :], in_sems.at[i, k])
                for i, ref in enumerate((first_ref, second_ref))
            ]
            for k in range(count)
        ]
        stores = [
            pltpu.make_async_copy(sums_ref.at[at[k], :], sum_ref.at[at[k], :], out_sems.at[k])
            for k in range(count)
        ]
        for pair in loads:
            for copy in pair:
                copy.start()
    else:
        (out_ref, total_ref), stores = refs, []
    core, chip, _ = position()
    for k in range(count):
        sources = [2 * (chip ^ k ^ far) + (core ^ side) for side in range(2) for far in (0, count)]
        index = jnp.concatenate([asked_ref[source] for source in sources], axis=1) - base
        rows = jnp.concatenate([grad_refs[k][...], grad_refs[count + k][...]], axis=0)
        add_segments(total_ref, index, rows, k == 0)
        if stores:
            for copy in loads[k]:
                copy.wait()
            here = slice(k * chunk, (k + 1) * chunk)
            terms = [terms_ref[i, here, :].astype(jnp.float32) for i in range(2)]
            sums_ref[here, :] = (terms[0] + terms[1]).astype(jnp.bfloat16)
            stores[k].start()
    put_segments(out_ref, total_ref)
    for copy in stores:
        copy.wait()


def row_gradients(asked, grads, peer_grads, base, row_count, terms=()):
    width = grads[0].shape[1]
    count = len(grads)
    split = SPLIT if row_count > 4 * 256 else SPLIT // 2
    anywhere = pl.BlockSpec(memory_space=pltpu.HBM)
    out_shape = [pltpu.VMEM((row_count, width), jnp.bfloat16)]
    scratch_shapes = [pltpu.VMEM((row_count // split, split * width), jnp.float32)]
    if terms:
        shape = terms[0].shape
        out_shape.append(jax.ShapeDtypeStruct(shape, jnp.bfloat16))
        scratch_shapes += [
            pltpu.VMEM((2,) + shape, jnp.bfloat16),
            pltpu.VMEM(shape, jnp.bfloat16),
            pltpu.SemaphoreType.DMA((2, count)),
            pltpu.SemaphoreType.DMA((count,)),
        ]
    return pl.pallas_call(
        functools.partial(segment_kernel, base=base, count=count),
        compiler_params=GRANT,
        in_specs=[VMEM] * (1 + 2 * count) + [anywhere] * len(terms),
        out_specs=[VMEM] + [anywhere] * (1 if terms else 0),
        out_shape=out_shape,
        scratch_shapes=scratch_shapes,
    )(near(asked), *[near(g, 2 * count) for g in (*grads, *peer_grads)], *terms)


def gather_kernel(asked_ref, table_ref, *refs, together):
    out_refs, (arrived_ref, held_ref, sems) = refs[:2], refs[2:]
    low_count, width = held_ref.shape[0], table_ref.shape[1]
    bags = asked_ref.shape[2]
    core, _, _ = position()
    copies = []
    for i in range(SPLIT):
        at = pl.ds(i * low_count, low_count)
        copies.append(pltpu.make_async_copy(table_ref.at[at, :], arrived_ref.at[at, :], sems.at[i]))
        copies[i].start()
    for i in range(SPLIT):
        copies[i].wait()
        rows = arrived_ref[i * low_count : (i + 1) * low_count, :]
        held_ref[:, i * width : (i + 1) * width] = rows.astype(jnp.bfloat16)
    lane = lax.broadcasted_iota(jnp.int32, (together * bags, width), 1)
    for side in (1, 0):
        for j in range(0, asked_ref.shape[0] // 2, together):
            index = jnp.concatenate(
                [asked_ref[2 * (j + i) + (core ^ side)] for i in range(together)], axis=1
            )
            block, low = split_index(column_of(index, width), low_count)
            hits = jnp.concatenate(
                [
                    (lane == low - first).astype(jnp.float32).astype(jnp.bfloat16)
                    for first in range(0, low_count, width)
                ],
                axis=1,
            )
            found = jnp.dot(hits, held_ref[...], preferred_element_type=jnp.float32)
            row = jnp.where(block == 0, found[:, :width], 0.0)
            for i in range(1, SPLIT):
                row = jnp.where(block == i, found[:, i * width : (i + 1) * width], row)
            out_refs[side][j * bags : (j + together) * bags, :] = row.astype(jnp.bfloat16)


def named_rows(asked, table):
    row_count, width = table.shape
    sources, _, bags = asked.shape
    rows = jax.ShapeDtypeStruct((sources // 2 * bags, width), jnp.bfloat16)
    return pl.pallas_call(
        functools.partial(gather_kernel, together=2),
        compiler_params=GRANT,
        in_specs=[VMEM, pl.BlockSpec(memory_space=pltpu.HBM)],
        out_specs=[VMEM, VMEM],
        out_shape=[rows, rows],
        scratch_shapes=[
            pltpu.VMEM(table.shape, table.dtype),
            pltpu.VMEM((row_count // SPLIT, SPLIT * width), jnp.bfloat16),
            pltpu.SemaphoreType.DMA((SPLIT,)),
        ],
    )(near(asked), table)


def diagonal_of(width):
    rows = lax.broadcasted_iota(jnp.int32, (width, width), 0)
    return rows == lax.broadcasted_iota(jnp.int32, (width, width), 1)


def fresh_accum_of(grads, accum_line, diagonal):
    width = grads.shape[1]
    rest, terms = grads * grads + jnp.where(diagonal, accum_line * width, 0.0), []
    for _ in range(3):
        terms.append(rest.astype(jnp.bfloat16))
        rest = rest - terms[-1].astype(jnp.float32)
    ones = jnp.ones((3 * width, width), jnp.bfloat16)
    sums = jnp.dot(jnp.concatenate(terms, axis=1), ones, preferred_element_type=jnp.float32)
    return sums * (1.0 / width)


def change_kernel(own_ref, other_ref, accum_ref, new_accum_ref, delta_ref, *, base):
    rows, width = own_ref.shape
    diagonal = diagonal_of(width)
    for j in range(rows // width):
        at = slice(j * width, (j + 1) * width)
        line = base // width + j
        grads = own_ref[at, :].astype(jnp.float32) + other_ref[at, :].astype(jnp.float32)
        fresh_accum = fresh_accum_of(grads, accum_ref[line : line + 1, :], diagonal)
        delta_ref[at, :] = (-LEARN * grads / jnp.sqrt(fresh_accum + EPSILON)).astype(jnp.bfloat16)
        new_accum_ref[j : j + 1, :] = jnp.sum(
            jnp.where(diagonal, fresh_accum, 0.0), axis=0, keepdims=True
        )


def changes_of(own, other, accum, base):
    rows, width = own.shape
    return pl.pallas_call(
        functools.partial(change_kernel, base=base),
        compiler_params=GRANT,
        in_specs=[VMEM] * 3,
        out_specs=[VMEM, VMEM],
        out_shape=[
            jax.ShapeDtypeStruct((rows // width, width), jnp.float32),
            pltpu.VMEM((rows, width), jnp.bfloat16),
        ],
    )(*map(near, (own, other, accum)))


def parity_kernel(*refs, base, holder_rows, dp_count, tile, last):
    slot_ref, peer_slot_ref, delta_ref, peer_delta_ref, table_ref = refs[:5]
    scratch, refs = refs[-5:], refs[5:-5]
    total_ref, old_ref, fresh_ref, load_sems, store_sems = scratch
    steps = delta_ref.shape[0] // tile
    if base > 0:
        start_ref, refs, held_ref, sem = refs[0], refs[2:-2], refs[-2], refs[-1]
        copy = pltpu.make_async_copy(start_ref, held_ref, sem)
        copy.start()
    new_table_ref, out_refs = refs[0], refs[1:]
    loads, stores = [], []
    for k in range(steps):
        here, there = pl.ds(k * tile, tile), pl.ds(base + k * tile, tile)
        loads.append(pltpu.make_async_copy(table_ref.at[there, :], old_ref.at[here, :], load_sems.at[k]))
        stores.append(
            pltpu.make_async_copy(fresh_ref.at[here, :], new_table_ref.at[there, :], store_sems.at[k])
        )
        loads[k].start()
    core, chip, dp_index = position()
    part_count = holder_rows // dp_count
    line_width = slot_ref.shape[1]
    width = delta_ref.shape[1]
    for k in range(steps):
        first = (base + k * tile) // line_width
        slot = jnp.concatenate(
            [
                ref[first + i : first + i + 1, :]
                for ref in (slot_ref, peer_slot_ref)
                for i in range(tile // line_width)
            ],
            axis=1,
        )
        holder, offset = split_index(slot, holder_rows)
        part, offset = split_index(offset, part_count)
        mine = (lax.bitwise_and(holder, 1) == core) & (part == dp_index)
        target = lax.bitwise_xor(lax.shift_right_arithmetic(holder, 1), chip) * part_count + offset
        at = slice(k * tile, (k + 1) * tile)
        rows = jnp.concatenate([delta_ref[at, :], peer_delta_ref[at, :]], axis=0)
        add_segments(total_ref, jnp.where(mine, target, -1), rows, k == 0)
        loads[k].wait()
        fresh_ref[at, :] = old_ref[at, :] + delta_ref[at, :].astype(jnp.float32)
        stores[k].start()
    if base > 0:
        copy.wait()
        total_ref[...] += held_ref[...]
    if last:
        low_count = total_ref.shape[0]
        for i, out_ref in enumerate(out_refs):
            block, low = divmod(i * part_count, low_count)
            out_ref[...] = total_ref[
                low : low + part_count, block * width : (block + 1) * width
            ].astype(out_ref.dtype)
    else:
        out_refs[0][...] = total_ref[...]
    for store in stores:
        store.wait()


def parity_changes(slot, peer_slot, delta, peer_delta, table, base, holder_rows, dp_count, chip_count, start, new_table, last):
    rows, width = delta.shape
    part_count = holder_rows // dp_count
    segment_count = chip_count * part_count
    held = pltpu.VMEM((segment_count // SPLIT, SPLIT * width), jnp.float32)
    anywhere = pl.BlockSpec(memory_space=pltpu.HBM)
    tile = min(1024, rows)
    changes = [pltpu.VMEM((part_count, width), jnp.bfloat16)] * chip_count
    if not last:
        changes = [jax.ShapeDtypeStruct(held.shape, held.dtype)]
    return pl.pallas_call(
        functools.partial(
            parity_kernel, base=base, holder_rows=holder_rows, dp_count=dp_count, tile=tile, last=last
        ),
        compiler_params=GRANT,
        in_specs=[VMEM] * 4 + [anywhere] * (1 + len(start) + len(new_table)),
        out_specs=[anywhere] + [VMEM] * len(changes),
        out_shape=[jax.ShapeDtypeStruct(table.shape, jnp.float32)] + changes,
        scratch_shapes=([held, pltpu.SemaphoreType.DMA] if start else [])
        + [
            held,
            pltpu.VMEM((rows, width), jnp.float32),
            pltpu.VMEM((rows, width), jnp.float32),
            pltpu.SemaphoreType.DMA((rows // tile,)),
            pltpu.SemaphoreType.DMA((rows // tile,)),
        ],
        input_output_aliases={6: 0} if new_table else {},
    )(*map(near, (slot, peer_slot, delta, peer_delta)), table, *start, *new_table)


def on_device(owners, local_rows, grad_pooled, table, accum, parity, parity_slot):
    table_count = lax.axis_size("table")
    dp_count = lax.axis_size("dp")
    chip_count = table_count // 2
    half = table_count // 2
    bag_count, _ = owners.shape
    row_count, width = table.shape
    parity_count = parity.shape[0]
    dp_index = lax.axis_index("dp")
    same_core = [list(range(c, table_count, 2)) for c in range(2)]

    def swap(values, distance):
        return lax.ppermute(values, "table", [(i, i ^ distance) for i in range(table_count)])

    def exchange(values):
        return lax.all_to_all(
            values, "table", split_axis=0, concat_axis=0, axis_index_groups=same_core, tiled=True
        )

    far_grads = swap(grad_pooled, half)

    devices = jnp.arange(table_count, dtype=jnp.int32)[:, None, None, None]
    named = owners.T[None, None] == devices
    requests = jnp.max(jnp.where(named, local_rows.T[None, None], -1), axis=2)
    asked = lax.all_to_all(requests, "table", split_axis=0, concat_axis=0, tiled=True)
    line_width = 4 * width
    slot_lines = parity_slot.reshape(-1, line_width)
    peer_slot_lines = swap(slot_lines, 1)

    grads = [jnp.concatenate([grad_pooled, far_grads], axis=0)]
    for k in range(1, chip_count // 2):
        grads.append(swap(grads[0], 2 * k))
    peer_grads = []
    for values in grads:
        peer_grads.append(swap(values, 1))

    own_named, peer_named = named_rows(asked, table)
    found = swap(peer_named, 1)

    fetched = (own_named.astype(jnp.float32) + found.astype(jnp.float32)).astype(jnp.bfloat16)

    halves, bases = [], []
    for part, share in enumerate(PARTS):
        part_rows = row_count // share
        bases.append(sum(row_count // other for other in PARTS[:part]))
        mine = row_gradients(asked, grads, peer_grads, bases[part], part_rows)[0]
        distance = 1
        other = lax.ppermute(mine, "dp", [(i, i ^ 1) for i in range(dp_count)])
        while 2 * distance < dp_count:
            distance *= 2
            mine = (mine.astype(jnp.float32) + other.astype(jnp.float32)).astype(jnp.bfloat16)
            other = lax.ppermute(mine, "dp", [(i, i ^ distance) for i in range(dp_count)])
        halves.append((mine, other))

    returned = exchange(fetched.reshape(chip_count, bag_count, width))

    accums, changes, new_table = [], [], []
    accum_lines = accum.reshape(-1, width)
    for part, (mine, other) in enumerate(halves):
        fresh_accum, delta = changes_of(mine, other, accum_lines, bases[part])
        accums.append(fresh_accum)
        peer_delta = swap(delta, 1)
        new_table, *changes = parity_changes(
            slot_lines, peer_slot_lines, delta, peer_delta, table, bases[part],
            parity_count, dp_count, chip_count, changes, new_table, part == len(PARTS) - 1,
        )
        new_table = [new_table]
    arrived = [changes[0]]
    for k in range(1, chip_count):
        arrived.append(swap(changes[k], 2 * k))
    pooled = jnp.sum(returned.astype(jnp.float32), axis=0).astype(jnp.bfloat16)
    new_accum = jnp.concatenate(accums, axis=0).reshape(row_count)
    part = sum(values.astype(jnp.float32) for values in arrived).astype(jnp.bfloat16)
    if dp_count == 2:
        other = lax.ppermute(part, "dp", [(0, 1), (1, 0)])
        parts = jnp.where(dp_index == 0, jnp.stack([part, other]), jnp.stack([other, part]))
    else:
        parts = lax.all_gather(part, "dp", axis=0)
    new_parity = parity + parts.reshape(parity_count, width).astype(jnp.float32)
    return (pooled, new_table[0], new_accum, new_parity)


def solution(mesh):
    in_specs = (
        P(("table", "dp"), None),
        P(("table", "dp"), None),
        P(("table", "dp"), None),
        P("table", None),
        P("table"),
        P("table", None),
        P("table"),
    )
    out_specs = (P(("table", "dp"), None), P("table", None), P("table"), P("table", None))

    return jax.shard_map(on_device, mesh=mesh, in_specs=in_specs, out_specs=out_specs, check_vma=False)
```
